32 devices in a mesh: tx: 4 (over x, core), ty: 4 (over z), solver: 2 (over y).
Axes of the slice: x: 2, y: 2, z: 4, core: 2. Of those that a mesh axis runs over, the one named last changes fastest.
Arguments:
- particle_state: float32 [8, 131072], P(None, ('tx', 'ty', 'solver')), as said below
- particle_cell: int32 [131072], P(('tx', 'ty', 'solver')), may hold values from 0 to 8191
- boundary_list: int32 [4, 4, 2, 2, 2, 256], P('tx', 'ty', 'solver'), may hold values from 0 to 4095
- boundary_count: int32 [4, 4, 2, 2, 2], P('tx', 'ty', 'solver'), may hold values from 128 to 256, as said below
- contact_own: int32 [4, 4, 2, 16384], P('tx', 'ty', 'solver'), may hold values from 0 to 4095
- contact_other: int32 [4, 4, 2, 16384], P('tx', 'ty', 'solver'), may hold values from 0 to 14335, as said below
- contact_count: int32 [4, 4, 2], P('tx', 'ty', 'solver'), may hold values from 1 to 16384, as said below
- gas_velocity: float32 [3, 16, 16, 512], P(None, 'solver', 'tx', 'ty'), may hold values from -6 to 6
- gas_source: float32 [3, 16, 16, 512], P(None, 'solver', 'tx', 'ty'), may hold values from -3 to 3
Outputs:
- particle_velocity: float32 [3, 131072], P(None, ('tx', 'ty', 'solver'))
- gas_velocity_new: float32 [3, 16, 16, 512], P(None, 'solver', 'tx', 'ty')
The draws below stay inside these ranges and needn't reach their ends.
Inputs may be any that keep to these rules, and one draw needn't show every extreme that they name: `boundary_count`: some quadrant list holds all 256 live entries. `contact_other`: never the tile column h * 4096 + contact_own of the same slot. The live slots of a device are its first contact_count; some device fills all 16384. `particle_state`: position rows in 0 to 1, radius in 0.3 to 0.7, mass in 0.5 to 2.
All inputs are finite; a program needn't handle non-finite values.
Results may differ from the reference program's by a relative error of at most 0.0003.
Values sent between devices are 32-bit elements; how exact they have to be, the bound alone decides.
A program may use at most 64 MiB of HBM per device.

```python
import jax
import jax.numpy as jnp
import numpy as np
from jax import lax

P_DEV = 4096
QUAD_LEN = 256
CX = 4
CY = 128
PAIR_TILES = 256
ITERS = 16
CONTACTS = 16384
NX = 16
NY = 512
NZ = 16
TILE_CELLS = 8192
TILE_COLS = 14336
PARTS_SIZE = 131072
N_TX = 4
N_TY = 4
N_SOLVER = 2


def draw_particle_state(key, part):
    key_list = jax.random.split(jax.random.fold_in(key, 17), 4)
    count_all = N_TX * N_TY * N_SOLVER * P_DEV
    position = jax.random.uniform(key_list[0], (3, count_all), jnp.float32, 0.0, 1.0)
    velocity = jax.random.normal(key_list[1], (3, count_all), jnp.float32)
    radius = jax.random.uniform(key_list[2], (1, count_all), jnp.float32, 0.3, 0.7)
    particle_mass = jnp.exp(jax.random.uniform(key_list[3], (1, count_all), jnp.float32, -0.6931, 0.6931))
    return jnp.concatenate([position, velocity, radius, particle_mass], axis=0)


def draw_boundary_count(key, part):
    count_key, place_key = jax.random.split(jax.random.fold_in(key, 19))
    shape_all = (N_TX, N_TY, N_SOLVER, 2, 2)
    counts = jax.random.randint(count_key, shape_all, QUAD_LEN // 2, QUAD_LEN + 1).reshape(-1)
    chosen = jax.random.randint(place_key, (), 0, counts.shape[0])
    return counts.at[chosen].set(QUAD_LEN).reshape(shape_all)


def contact_pairs(key):
    own_key, step_key = jax.random.split(jax.random.fold_in(key, 11))
    shape_all = (N_TX, N_TY, N_SOLVER, CONTACTS)
    own_rows = jax.random.randint(own_key, shape_all, 0, P_DEV)
    stride = jax.random.randint(step_key, shape_all, 0, TILE_COLS - 1)
    half_rows = lax.broadcasted_iota(jnp.int32, shape_all, 2)
    other_rows = (half_rows * P_DEV + own_rows + 1 + stride) % TILE_COLS
    return (own_rows, other_rows)


def draw_contact_own(key, part):
    return contact_pairs(key)[0]


def draw_contact_other(key, part):
    return contact_pairs(key)[1]


def draw_contact_count(key, part):
    shift_key, trim_key, place_key = jax.random.split(jax.random.fold_in(key, 13), 3)
    shape_all = (N_TX, N_TY, N_SOLVER)
    shift_amount = jax.random.randint(shift_key, shape_all, 0, 4)
    live_tiles = jnp.maximum(jnp.right_shift(jnp.full(shape_all, PAIR_TILES, jnp.int32), shift_amount), 1)
    trimmed = jax.random.randint(trim_key, shape_all, 0, 64)
    counts = jnp.maximum(live_tiles * 64 - trimmed, 1).reshape(-1)
    chosen = jax.random.randint(place_key, (), 0, counts.shape[0])
    return counts.at[chosen].set(CONTACTS).reshape(shape_all)


def with_ends(result, stream_key, least, high):
    longest = result.shape.index(max(result.shape))
    spots = []
    for shift in (0, 1):
        where = [jax.random.randint(jax.random.fold_in(stream_key, axis), (), 0, length) for axis, length in enumerate(result.shape)]
        where[longest] = (where[longest] + shift) % result.shape[longest]
        spots.append(tuple(where))
    return result.at[spots[0]].set(least).at[spots[1]].set(high)


def shard_levels(stream_key, extent, cuts, low, largest):
    factor_of = 1.0
    for dim, shards_of in cuts:
        draws = jax.random.uniform(jax.random.fold_in(jax.random.fold_in(stream_key, 6), dim), (shards_of,), jnp.float32, low / len(cuts), largest / len(cuts))
        factor_of = factor_of * jnp.repeat(jnp.exp(draws), extent[dim] // shards_of).reshape((-1,) + (1,) * (len(extent) - 1 - dim))
    return factor_of


def centred(rng, extent, scale, bound, shards=(), kind=jnp.bfloat16):
    level = shard_levels(rng, extent, shards, -0.22, 0.18) if shards else 1.0
    values = jax.random.normal(rng, extent, jnp.float32) * scale * level
    return jnp.minimum(jnp.maximum(values, -bound), bound).astype(kind)


def setup_inputs(seed: int = 0) -> dict:
    arg_keys = jax.random.split(jax.random.key(seed), 10)
    return {
        "particle_state": draw_particle_state(jax.random.fold_in(arg_keys[9], 71), 0),
        "particle_cell": with_ends(jax.random.randint(arg_keys[1], (PARTS_SIZE,), 0, TILE_CELLS), jax.random.fold_in(arg_keys[1], 1), 0, TILE_CELLS - 1).astype(jnp.int32),
        "boundary_list": with_ends(jax.random.randint(arg_keys[2], (N_TX, N_TY, N_SOLVER, 2, 2, QUAD_LEN), 0, P_DEV), jax.random.fold_in(arg_keys[2], 1), 0, P_DEV - 1).astype(jnp.int32),
        "boundary_count": draw_boundary_count(jax.random.fold_in(arg_keys[9], 71), 0),
        "contact_own": draw_contact_own(jax.random.fold_in(arg_keys[9], 71), 0),
        "contact_other": draw_contact_other(jax.random.fold_in(arg_keys[9], 71), 0),
        "contact_count": draw_contact_count(jax.random.fold_in(arg_keys[9], 71), 0),
        "gas_velocity": centred(arg_keys[7], (3, NZ, NX, NY), 1.0, 6.0, ((1, 2), (2, 4), (3, 4)), jnp.float32),
        "gas_source": centred(arg_keys[8], (3, NZ, NX, NY), 0.5, 3.0, ((1, 2), (2, 4), (3, 4)), jnp.float32),
    }


FAR = 100.0
STIFF = 4.0
DAMPING = 1.0
FLOOR = 0.1
BETA_RATE = 2.0
VOLUME = 4.18879
TIME_STEP = 0.1
GRAVITY = 1.0
VISCOSITY = 1.0

def cycle_layout():
    shifts = [-1, 0, 0, 1]
    slot_list = []
    x_shift = []
    y_shift = []
    for row_pos in range(4):
        for col_pos in range(4):
            if row_pos in (1, 2) and col_pos in (1, 2):
                continue
            slot_list.append(row_pos * 4 + col_pos)
            x_shift.append(shifts[row_pos])
            y_shift.append(shifts[col_pos])
    offsets = np.zeros((8, len(slot_list), 1), np.float32)
    offsets[0, :, 0] = x_shift
    offsets[1, :, 0] = y_shift
    return (np.array(slot_list), offsets)

def pick_quadrants(state, lists, counts):
    list_width = lists.shape[-1]
    picked = jnp.take(state, lists.reshape(-1), axis=1).reshape(8, 2, 2, list_width)
    live_mask = jnp.arange(list_width, dtype=jnp.int32)[None, None, :] < counts[:, :, None]
    filler = jnp.array([FAR, FAR, FAR, 0.0, 0.0, 0.0, 0.0, 0.0], state.dtype)[:, None, None, None]
    return jnp.where(live_mask[None], picked, filler)

def pair_force(first_cols, second):
    separation = first_cols[0:3] - second[0:3]
    distance = jnp.sqrt(lax.optimization_barrier(jnp.sum(separation * separation, axis=0)))
    normal = separation / jnp.maximum(distance, FLOOR)
    intersection = jnp.maximum(first_cols[6] + second[6] - distance, 0.0)
    closing = lax.optimization_barrier(jnp.sum((first_cols[3:6] - second[3:6]) * normal, axis=0))
    root_intersection = jnp.sqrt(intersection)
    magnitude = STIFF * intersection * root_intersection - DAMPING * root_intersection * closing
    return magnitude * normal

def coupling_terms(state):
    radius = state[6]
    drag_rate = BETA_RATE * radius
    return jnp.concatenate([(VOLUME * radius ** 3)[None], drag_rate[None], drag_rate[None] * state[3:6]], axis=0)

def advance(state, forces, gas_cells, cells):
    at_cell = jnp.take(gas_cells, cells, axis=1)
    velocity = state[3:6]
    drag_rate = BETA_RATE * state[6]
    gravity = jnp.array([0.0, 0.0, -GRAVITY], state.dtype)[:, None]
    return velocity + TIME_STEP * (forces + drag_rate * (at_cell - velocity)) / state[7] + TIME_STEP * gravity

def grow_grid(quadrants):
    shifts = [-1, 0, 0, 1]
    row_list = []
    for row_pos in range(4):
        column_list = []
        for col_pos in range(4):
            part_x = (row_pos + 1) % 2
            part_y = (col_pos + 1) % 2
            shifted_grid = jnp.roll(quadrants[:, :, :, :, part_x, part_y, :], (-shifts[row_pos], -shifts[col_pos]), axis=(0, 1))
            column_list.append(shifted_grid)
        row_list.append(jnp.stack(column_list, axis=4))
    return jnp.stack(row_list, axis=4)

def reference(particle_state, particle_cell, boundary_list, boundary_count, contact_own, contact_other, contact_count, gas_velocity, gas_source):
    halves = N_SOLVER
    states = jnp.moveaxis(particle_state.reshape(8, N_TX, N_TY, halves, P_DEV), 0, 3)
    quadrants = jax.vmap(jax.vmap(jax.vmap(pick_quadrants)))(states, boundary_list, boundary_count)
    grown_grid = grow_grid(quadrants)
    slot_list, offsets = cycle_layout()
    cycle_cols = grown_grid.reshape(N_TX, N_TY, halves, 8, 16, QUAD_LEN)[:, :, :, :, slot_list, :]
    cycle_cols = (cycle_cols + jnp.asarray(offsets, particle_state.dtype)).reshape(N_TX, N_TY, halves, 8, 12 * QUAD_LEN)
    own_part = jnp.moveaxis(states, 2, 3).reshape(N_TX, N_TY, 8, halves * P_DEV)
    cycle_part = jnp.moveaxis(cycle_cols, 2, 3).reshape(N_TX, N_TY, 8, halves * 12 * QUAD_LEN)
    tile_data = jnp.concatenate([own_part, cycle_part], axis=3).reshape(N_TX * N_TY, 8, TILE_COLS)
    gas_tiles = gas_velocity.reshape(3, NZ, N_TX, CX, N_TY, CY).transpose(2, 4, 0, 1, 3, 5).reshape(N_TX * N_TY, 3, TILE_CELLS)
    state_tiles = states.reshape(N_TX * N_TY, halves, 8, P_DEV)
    cell_tiles = particle_cell.reshape(N_TX * N_TY, halves, P_DEV)
    own_tiles = contact_own.reshape(N_TX * N_TY, halves, CONTACTS)
    other_tiles = contact_other.reshape(N_TX * N_TY, halves, CONTACTS)
    count_tiles = contact_count.reshape(N_TX * N_TY, halves)

    def tile_step(packed):
        tile_one, gas_one, state_pair, cell_pair, own_pair, other_pair, count_pair = packed
        binned = jnp.zeros((5, TILE_CELLS), tile_one.dtype)
        new_velocity = []
        for half_index in range(halves):
            first_cols = jnp.take(tile_one, half_index * P_DEV + own_pair[half_index], axis=1)
            second = jnp.take(tile_one, other_pair[half_index], axis=1)
            live_mask = (jnp.arange(CONTACTS, dtype=jnp.int32) < count_pair[half_index]).astype(tile_one.dtype)
            pushed = pair_force(first_cols, second) * live_mask
            forces = jnp.zeros((3, P_DEV), tile_one.dtype).at[:, own_pair[half_index]].add(pushed)
            new_velocity.append(advance(state_pair[half_index], forces, gas_one, cell_pair[half_index]))
            binned = binned.at[:, cell_pair[half_index]].add(coupling_terms(state_pair[half_index]))
        return (jnp.stack(new_velocity), binned)
    moved_all, binned_all = lax.map(tile_step, (tile_data, gas_tiles, state_tiles, cell_tiles, own_tiles, other_tiles, count_tiles))
    particle_velocity = moved_all.transpose(2, 0, 1, 3).reshape(3, PARTS_SIZE)
    coupled = binned_all.reshape(N_TX, N_TY, 5, NZ, CX, CY).transpose(2, 3, 0, 4, 1, 5).reshape(5, NZ, NX, NY)
    porous = 1.0 / (1.0 + coupled[0])
    rhs_gas = porous * gas_velocity + coupled[2:5] + gas_source
    diagonal = porous + coupled[1] + 6.0 * VISCOSITY
    gas_field = gas_velocity
    for sweep_index in range(ITERS):
        padded = jnp.pad(gas_field, ((0, 0), (1, 1), (0, 0), (0, 0)))
        beside = padded[:, 2:] + padded[:, :-2]
        beside = beside + jnp.roll(gas_field, 1, 2) + jnp.roll(gas_field, -1, 2)
        beside = beside + jnp.roll(gas_field, 1, 3) + jnp.roll(gas_field, -1, 3)
        gas_field = (rhs_gas + VISCOSITY * beside) / diagonal
    return (particle_velocity, gas_field)
```

```python
import functools

import jax
import jax.numpy as jnp
from jax import lax
from jax.experimental import pallas as pl
from jax.experimental.pallas import tpu as pltpu
from jax.sharding import PartitionSpec as P

ITERS = 16
FAR = 100.0
STIFF = 4.0
DAMPING = 1.0
FLOOR = 0.1
BETA_RATE = 2.0
VOLUME = 4.18879
TIME_STEP = 0.1
GRAVITY = 1.0
VISCOSITY = 1.0
SUB = 8
LANES = 128
HALO = 16
PAIR_ROWS = 32
SHIFTS = (-1, 0, 0, 1)
SLOTS = tuple((a, b) for a in range(4) for b in range(4) if not (a in (1, 2) and b in (1, 2)))
VMEM_LIMIT = 48 << 20
MESH = pl.DeviceIdType.MESH
F32 = jnp.float32


def vmem_specs(count):
    return [pl.BlockSpec(memory_space=pltpu.VMEM)] * count


def lane_take(row, low):
    return jnp.take_along_axis(jnp.broadcast_to(row, low.shape), low, axis=1, mode="promise_in_bounds")


def take_groups(load_row, rows, groups, high, low, unroll):
    chunks = high[0].shape
    start = tuple(jnp.zeros(chunks, F32) for _ in range(len(high) * len(rows)))

    def step(group, acc):
        out = []
        table = [load_row(r, group) for r in rows]
        for i in range(len(high)):
            hit = high[i] == group
            for j in range(len(rows)):
                out.append(jnp.where(hit, lane_take(table[j], low[i]), acc[i * len(rows) + j]))
        return tuple(out)

    flat = lax.fori_loop(0, groups, step, start, unroll=unroll)
    return [flat[i * len(rows) : (i + 1) * len(rows)] for i in range(len(high))]


def two_parts(value):
    high = value.astype(jnp.bfloat16).astype(F32)
    return (high, value - high)


def spread_dot(values, high, low, high_count):
    row_count = high.shape[0]
    parts = []
    for value in values:
        parts.extend(two_parts(value))
    lefts = []
    rights = []
    high_iota = lax.broadcasted_iota(jnp.int32, (high_count, LANES), 0)
    low_iota = lax.broadcasted_iota(jnp.int32, (LANES, LANES), 0)
    for s in range(row_count):
        hit = jnp.broadcast_to(high[s : s + 1], (high_count, LANES)) == high_iota
        left = [
            jnp.where(hit, jnp.broadcast_to(part[s : s + 1], (high_count, LANES)), 0.0).astype(jnp.bfloat16)
            for part in parts
        ]
        lefts.append(jnp.concatenate(left, axis=0))
        right = jnp.broadcast_to(low[s : s + 1], (LANES, LANES)) == low_iota
        rights.append(jnp.where(right, 1.0, 0.0).astype(jnp.bfloat16))
    left = jnp.concatenate(lefts, axis=1)
    right = jnp.concatenate(rights, axis=1)
    out = lax.dot_general(left, right, (((1,), (1,)), ((), ())), preferred_element_type=F32)
    sums = []
    for i in range(len(values)):
        base = 2 * i * high_count
        sums.append(out[base : base + high_count] + out[base + high_count : base + 2 * high_count])
    return sums


def pack_edges(rows):
    lane = lax.broadcasted_iota(jnp.int32, rows[0].shape, 1)
    half = LANES // 2
    packed = jnp.zeros(rows[0].shape, F32)
    for x, row in enumerate(rows):
        left = pltpu.roll(row, (x * HALO) % LANES, axis=1)
        right = pltpu.roll(row, (half + x * HALO + HALO) % LANES, axis=1)
        packed = jnp.where((lane >= x * HALO) & (lane < x * HALO + HALO), left, packed)
        base = half + x * HALO
        packed = jnp.where((lane >= base) & (lane < base + HALO), right, packed)
    return packed


def local_kernel(
    levels_all, rows_x,
    count_ref, state_ref, cell_ref, list_ref, gas_ref, source_ref,
    ghost_ref, bins_ref, field_ref, src_ref, edge_ref,
):
    groups = state_ref.shape[1] // LANES
    index = list_ref[...]
    picked = take_groups(
        lambda r, g: state_ref[r : r + 1, pl.ds(pl.multiple_of(g * LANES, LANES), LANES)],
        range(8), groups, [index >> 7], [index & 127], 4,
    )[0]
    lines = index.shape[0] // 4
    row_iota = lax.broadcasted_iota(jnp.int32, index.shape, 0)
    place = (row_iota % lines) * LANES + lax.broadcasted_iota(jnp.int32, index.shape, 1)
    quad = row_iota // lines
    limit = jnp.zeros(index.shape, jnp.int32)
    for q in range(4):
        limit = jnp.where(quad == q, count_ref[q], limit)
    live = place < limit
    width = lines * LANES
    for r in range(8):
        value = jnp.where(live, picked[r], FAR if r < 3 else 0.0)
        for s, (a, b) in enumerate(SLOTS):
            q = ((a + 1) % 2) * 2 + (b + 1) % 2
            shift = SHIFTS[a] if r == 0 else SHIFTS[b] if r == 1 else 0
            for line in range(lines):
                row = value[q * lines + line : q * lines + line + 1]
                if r < 2:
                    row = row + float(shift)
                base = s * width + line * LANES
                ghost_ref[r : r + 1, base : base + LANES] = row

    high_count = rows_x * levels_all
    totals = None
    for block in range(groups // SUB):
        rows = [
            jnp.concatenate(
                [
                    state_ref[r : r + 1, (block * SUB + s) * LANES : (block * SUB + s + 1) * LANES]
                    for s in range(SUB)
                ],
                axis=0,
            )
            for r in (3, 4, 5, 6)
        ]
        radius = rows[3]
        drag = BETA_RATE * radius
        values = [VOLUME * radius * radius * radius, drag] + [drag * rows[c] for c in range(3)]
        cell = cell_ref[block * SUB : (block + 1) * SUB, :]
        line = cell >> 7
        high = (line % rows_x) * levels_all + line // rows_x
        sums = spread_dot(values, high, cell & 127, high_count)
        totals = sums if totals is None else [t + s for t, s in zip(totals, sums)]
    for p in range(5):
        bins_ref[p] = totals[p].reshape(rows_x, levels_all, LANES)
    for c in range(3):
        rows = []
        for x in range(rows_x):
            row = gas_ref[c, :, x, :]
            rows.append(row)
            field_ref[c, x] = row
            src_ref[c, x] = source_ref[c, :, x, :]
        edge_ref[c] = pack_edges(rows)


def exchange_kernel(
    sizes,
    state_ref, ghost_ref, bins_ref, field_ref, src_ref, edge_ref,
    tile_ref, gas_all, rhs_all, above_gas, below_gas, above_rhs, below_rhs,
    bins_in, mine, mine_edge, send_sem, recv_sem,
):
    n_x, n_y, n_h = sizes
    x, y, h = (lax.axis_index(name) for name in ("tx", "ty", "solver"))
    levels = field_ref.shape[2]
    rows_x = field_ref.shape[1]
    own = state_ref.shape[1]
    ring = n_x * n_h
    me = x * n_h + h
    barrier = pltpu.get_barrier_semaphore()
    up = (y + 1) % n_y
    down = (y + n_y - 1) % n_y

    def member(step):
        spot = (me + step) % ring
        return spot // n_h, spot % n_h

    for step in range(ring):
        t, k = member(step)
        for line in ((y, up, down) if step else (up, down)):
            pl.semaphore_signal(barrier, inc=1, device_id=(t, line, k), device_id_type=MESH)
    pl.semaphore_wait(barrier, 3 * ring - 1)

    copies = []

    def send(src, dst, kind, target):
        copy = pltpu.make_async_remote_copy(
            src_ref=src, dst_ref=dst, send_sem=send_sem.at[len(copies)], recv_sem=recv_sem.at[kind],
            device_id=target, device_id_type=MESH,
        )
        copy.start()
        copies.append(copy)

    def keep(src, dst, kind):
        pltpu.make_async_copy(src, dst, recv_sem.at[kind]).start()

    partner = (h + 1) % n_h
    theirs = pl.multiple_of(partner * levels, levels)
    here = pl.multiple_of(h * levels, levels)
    send(bins_ref.at[:, :, pl.ds(theirs, levels), :], bins_in, 0, (x, y, partner))
    state_at = tile_ref.at[:, pl.ds(pl.multiple_of(h * own, own), own)]
    send(state_ref, state_at, 1, (x, y, partner))
    keep(state_ref, state_at, 1)
    cycle = ghost_ref.shape[1]
    width = cycle // len(SLOTS)
    base = n_h * own + h * cycle
    runs = ((0, 1), (1, 2), (3, 1), (4, 1), (5, 1), (6, 1), (7, 1), (8, 1), (9, 2), (11, 1))
    for first, length in runs:
        a, b = SLOTS[first]
        to_x = (x + n_x - SHIFTS[a]) % n_x
        to_y = (y + n_y - SHIFTS[b]) % n_y
        src = ghost_ref.at[:, first * width : (first + length) * width]
        dst = tile_ref.at[:, pl.ds(pl.multiple_of(base + first * width, width), length * width)]
        for k in range(n_h):
            send(src, dst, 1, (to_x, to_y, (h + k) % n_h))

    def gather(block, edges, whole, above, below, kinds):
        spot = whole.at[:, pl.ds(x * rows_x, rows_x), pl.ds(here, levels), :]
        keep(block, spot, kinds)
        for step in range(1, ring):
            t, k = member(step)
            send(block, spot, kinds, (t, y, k))
        for step in range(ring):
            t, k = member(step)
            send(edges, above.at[:, x, pl.ds(here, levels), :], kinds + 1, (t, down, k))
            send(edges, below.at[:, x, pl.ds(here, levels), :], kinds + 2, (t, up, k))

    gather(field_ref, edge_ref, gas_all, above_gas, below_gas, 2)
    pltpu.make_async_copy(bins_in, bins_in, recv_sem.at[0]).wait()
    edge_rows = [[], [], [], []]
    for i in range(rows_x):
        sums = [bins_ref[p, i, pl.ds(here, levels), :] + bins_in[p, i] for p in range(5)]
        porous = 1.0 / (1.0 + sums[0])
        inverse = 1.0 / (porous + sums[1] + 6.0 * VISCOSITY)
        values = [porous * field_ref[c, i] + sums[2 + c] + src_ref[c, i] for c in range(3)] + [inverse]
        for p in range(4):
            mine[p, i] = values[p]
            edge_rows[p].append(values[p])
    for p in range(4):
        mine_edge[p] = pack_edges(edge_rows[p])
    gather(mine, mine_edge, rhs_all, above_rhs, below_rhs, 5)
    for kind, ref in enumerate((tile_ref, gas_all, above_gas, below_gas, rhs_all, above_rhs, below_rhs)):
        pltpu.make_async_copy(ref, ref, recv_sem.at[kind + 1]).wait()
    for copy in copies:
        copy.wait_send()


def pair_kernel(
    rows_x,
    count_ref, tile_ref, state_ref, state_rows, cell_ref, own_ref, other_ref, gas_all,
    out_ref, force_ref,
):
    levels_all = gas_all.shape[2]
    x = lax.axis_index("tx")
    groups = state_ref.shape[1] // LANES
    tile_groups = tile_ref.shape[1] // LANES
    force_ref[...] = jnp.zeros_like(force_ref)
    count = count_ref[0]
    block = PAIR_ROWS * LANES
    chunks = PAIR_ROWS // SUB

    @pl.loop(0, (count + block - 1) // block)
    def _(round_index):
        start = pl.multiple_of(round_index * PAIR_ROWS, PAIR_ROWS)
        own = [own_ref[pl.ds(start + i * SUB, SUB), :] for i in range(chunks)]
        other = [other_ref[pl.ds(start + i * SUB, SUB), :] for i in range(chunks)]
        rows = range(7)
        first = take_groups(
            lambda r, g: state_ref[r : r + 1, pl.ds(pl.multiple_of(g * LANES, LANES), LANES)],
            rows, groups, [v >> 7 for v in own], [v & 127 for v in own], 2,
        )
        second = take_groups(
            lambda r, g: tile_ref[r : r + 1, pl.ds(pl.multiple_of(g * LANES, LANES), LANES)],
            rows, tile_groups, [v >> 7 for v in other], [v & 127 for v in other], 2,
        )
        for i in range(chunks):
            a, b = first[i], second[i]
            gap = [a[c] - b[c] for c in range(3)]
            distance = jnp.sqrt(gap[0] * gap[0] + gap[1] * gap[1] + gap[2] * gap[2])
            scale = 1.0 / jnp.maximum(distance, FLOOR)
            normal = [v * scale for v in gap]
            overlap = jnp.maximum(a[6] + b[6] - distance, 0.0)
            closing = sum((a[3 + c] - b[3 + c]) * normal[c] for c in range(3))
            root = jnp.sqrt(overlap)
            size = STIFF * overlap * root - DAMPING * root * closing
            place = (
                (start + i * SUB + lax.broadcasted_iota(jnp.int32, (SUB, LANES), 0)) * LANES
                + lax.broadcasted_iota(jnp.int32, (SUB, LANES), 1)
            )
            size = jnp.where(place < count, size, 0.0)
            sums = spread_dot([size * v for v in normal], own[i] >> 7, own[i] & 127, groups)
            for c in range(3):
                force_ref[c] += sums[c]

    for i in range(groups // SUB):
        cell = cell_ref[i * SUB : (i + 1) * SUB, :]
        line = cell >> 7
        high = (line % rows_x) * levels_all + line // rows_x
        at_cell = take_groups(
            lambda c, g: gas_all[c, x * rows_x + g // levels_all, pl.ds(g % levels_all, 1), :],
            range(3), rows_x * levels_all, [high], [cell & 127], 4,
        )[0]
        span = slice(i * SUB, (i + 1) * SUB)
        drag = BETA_RATE * state_rows[6, span, :]
        rate = TIME_STEP / state_rows[7, span, :]
        for c in range(3):
            velocity = state_rows[3 + c, span, :]
            value = velocity + (force_ref[c, span, :] + drag * (at_cell[c] - velocity)) * rate
            if c == 2:
                value = value - TIME_STEP * GRAVITY
            out_ref[c, span, :] = value


def sweep_kernel(
    rows_x,
    gas_all, rhs_all, above_gas, below_gas, above_rhs, below_rhs,
    out_ref, field_a, field_b, rhs_ref,
):
    n_all, levels_all = gas_all.shape[1], gas_all.shape[2]
    levels = out_ref.shape[1]
    x, h = lax.axis_index("tx"), lax.axis_index("solver")
    lane = lax.broadcasted_iota(jnp.int32, (levels_all, LANES), 1)

    def fill(planes, whole, above, below, target):
        @pl.loop(0, n_all // rows_x)
        def _(t):
            for p in range(planes):
                high = above[p, t]
                low = below[p, t]
                for i in range(rows_x):
                    at = t * rows_x + i
                    target[p, at, :, 0:LANES] = whole[p, at]
                    right = pltpu.roll(high, (LANES - i * HALO) % LANES, axis=1)
                    left = pltpu.roll(low, (LANES // 2 - (i + 1) * HALO) % LANES, axis=1)
                    edge = jnp.where(lane < HALO, right, jnp.where(lane >= LANES - HALO, left, 0.0))
                    target[p, at, :, LANES : 2 * LANES] = edge

    fill(3, gas_all, above_gas, below_gas, field_a)
    fill(4, rhs_all, above_rhs, below_rhs, rhs_ref)
    level = lax.broadcasted_iota(jnp.int32, (levels_all, 2 * LANES), 0)

    def sweep(source, target):
        @pl.loop(0, n_all // 2)
        def _(pair):
            for j in range(2):
                at = pair * 2 + j
                inverse = rhs_ref[3, at]
                for c in range(3):
                    mid = source[c, at]
                    total = rhs_ref[c, at] + source[c, (at + 1) % n_all] + source[c, (at + n_all - 1) % n_all]
                    total = total + jnp.where(level == 0, 0.0, pltpu.roll(mid, 1, axis=0))
                    total = total + jnp.where(level == levels_all - 1, 0.0, pltpu.roll(mid, levels_all - 1, axis=0))
                    total = total + pltpu.roll(mid, 1, axis=1) + pltpu.roll(mid, 2 * LANES - 1, axis=1)
                    target[c, at] = total * inverse

    @pl.loop(0, ITERS // 2)
    def _(step):
        sweep(field_a, field_b)
        sweep(field_b, field_a)

    here = pl.multiple_of(h * levels, levels)
    for c in range(3):
        for i in range(rows_x):
            out_ref[c, :, i, :] = field_a[c, x * rows_x + i, pl.ds(here, levels), 0:LANES]


def on_device(
    sizes,
    particle_state, particle_cell, boundary_list, boundary_count,
    contact_own, contact_other, contact_count, gas_velocity, gas_source,
):
    n_x, n_y, n_h = sizes
    own = particle_state.shape[1]
    levels, rows_x, rows_y = gas_velocity.shape[1:]
    levels_all = levels * n_h
    width = boundary_list.shape[-1]
    cycle = len(SLOTS) * width
    shape = lambda *dims: jax.ShapeDtypeStruct(dims, F32)
    smem = pl.BlockSpec(memory_space=pltpu.SMEM)
    params = functools.partial(pltpu.CompilerParams, vmem_limit_bytes=VMEM_LIMIT)
    cells = particle_cell.reshape(-1, LANES)
    ghosts, bins, field, source, edges = pl.pallas_call(
        functools.partial(local_kernel, levels_all, rows_x),
        out_shape=(
            shape(8, cycle), shape(5, rows_x, levels_all, rows_y), shape(3, rows_x, levels, rows_y),
            shape(3, rows_x, levels, rows_y), shape(3, levels, LANES),
        ),
        in_specs=[smem] + vmem_specs(5),
        out_specs=tuple(vmem_specs(5)),
        compiler_params=params(),
        name="local",
    )(
        boundary_count.reshape(4), particle_state, cells, boundary_list.reshape(-1, LANES),
        gas_velocity, gas_source,
    )
    n_all = n_x * rows_x
    ring = n_x * n_h
    sends = 2 + 10 * n_h + 2 * (ring - 1 + 2 * ring)
    tile, gas_all, rhs_all, above_gas, below_gas, above_rhs, below_rhs = pl.pallas_call(
        functools.partial(exchange_kernel, sizes),
        out_shape=(
            shape(8, n_h * (own + cycle)),
            shape(3, n_all, levels_all, rows_y), shape(4, n_all, levels_all, rows_y),
            shape(3, n_x, levels_all, LANES), shape(3, n_x, levels_all, LANES),
            shape(4, n_x, levels_all, LANES), shape(4, n_x, levels_all, LANES),
        ),
        in_specs=vmem_specs(6),
        out_specs=tuple(vmem_specs(7)),
        scratch_shapes=[
            pltpu.VMEM((5, rows_x, levels, rows_y), F32),
            pltpu.VMEM((4, rows_x, levels, rows_y), F32),
            pltpu.VMEM((4, levels, LANES), F32),
            pltpu.SemaphoreType.DMA((sends,)),
            pltpu.SemaphoreType.DMA((8,)),
        ],
        compiler_params=params(collective_id=0, has_side_effects=True),
        name="exchange",
    )(particle_state, ghosts, bins, field, source, edges)
    moved = pl.pallas_call(
        functools.partial(pair_kernel, rows_x),
        out_shape=shape(3, own // LANES, LANES),
        in_specs=[smem] + vmem_specs(7),
        out_specs=vmem_specs(1)[0],
        scratch_shapes=[pltpu.VMEM((3, own // LANES, LANES), F32)],
        compiler_params=params(),
        name="pairs",
    )(
        contact_count.reshape(1), tile, particle_state, particle_state.reshape(8, -1, LANES), cells,
        contact_own.reshape(-1, LANES), contact_other.reshape(-1, LANES), gas_all,
    )
    swept = pl.pallas_call(
        functools.partial(sweep_kernel, rows_x),
        out_shape=shape(3, levels, rows_x, rows_y),
        in_specs=vmem_specs(6),
        out_specs=vmem_specs(1)[0],
        scratch_shapes=[
            pltpu.VMEM((3, n_all, levels_all, 2 * LANES), F32),
            pltpu.VMEM((3, n_all, levels_all, 2 * LANES), F32),
            pltpu.VMEM((4, n_all, levels_all, 2 * LANES), F32),
        ],
        compiler_params=params(),
        name="sweeps",
    )(gas_all, rhs_all, above_gas, below_gas, above_rhs, below_rhs)
    return (moved.reshape(3, own), swept)


def solution(mesh):
    sizes = (mesh.shape["tx"], mesh.shape["ty"], mesh.shape["solver"])
    in_specs = (
        P(None, ("tx", "ty", "solver")),
        P(("tx", "ty", "solver")),
        P("tx", "ty", "solver", None, None, None),
        P("tx", "ty", "solver", None, None),
        P("tx", "ty", "solver", None),
        P("tx", "ty", "solver", None),
        P("tx", "ty", "solver"),
        P(None, "solver", "tx", "ty"),
        P(None, "solver", "tx", "ty"),
    )
    out_specs = (P(None, ("tx", "ty", "solver")), P(None, "solver", "tx", "ty"))
    return jax.shard_map(
        functools.partial(on_device, sizes), mesh=mesh, in_specs=in_specs, out_specs=out_specs, check_vma=False
    )
```

```python
import functools

import jax
import jax.numpy as jnp
from jax import lax
from jax.experimental import pallas as pl
from jax.experimental.pallas import tpu as pltpu
from jax.sharding import PartitionSpec as P

ITERS = 16
FAR = 100.0
STIFF = 4.0
DAMPING = 1.0
FLOOR = 0.1
BETA_RATE = 2.0
VOLUME = 4.18879
TIME_STEP = 0.1
GRAVITY = 1.0
VISCOSITY = 1.0
SUB = 8
LANES = 128
HALO = 16
SHIFTS = (-1, 0, 0, 1)
SLOTS = tuple((a, b) for a in range(4) for b in range(4) if not (a in (1, 2) and b in (1, 2)))
VMEM_LIMIT = 48 << 20
MESH = pl.DeviceIdType.MESH
F32 = jnp.float32


def vmem_specs(count):
    return [pl.BlockSpec(memory_space=pltpu.VMEM)] * count


def lane_take(row, low):
    return jnp.take_along_axis(jnp.broadcast_to(row, low.shape), low, axis=1, mode="promise_in_bounds")


def take_groups(load_row, rows, groups, high, low, unroll):
    chunks = high[0].shape
    start = tuple(jnp.zeros(chunks, F32) for _ in range(len(high) * len(rows)))

    def step(group, acc):
        out = []
        table = [load_row(r, group) for r in rows]
        for i in range(len(high)):
            hit = high[i] == group
            for j in range(len(rows)):
                out.append(jnp.where(hit, lane_take(table[j], low[i]), acc[i * len(rows) + j]))
        return tuple(out)

    flat = lax.fori_loop(0, groups, step, start, unroll=unroll)
    return [flat[i * len(rows) : (i + 1) * len(rows)] for i in range(len(high))]


def two_parts(value):
    high = value.astype(jnp.bfloat16).astype(F32)
    return (high, value - high)


def spread_dot(values, high, low, high_count):
    row_count = high.shape[0]
    parts = []
    for value in values:
        parts.extend(two_parts(value))
    lefts = []
    rights = []
    high_iota = lax.broadcasted_iota(jnp.int32, (high_count, LANES), 0)
    low_iota = lax.broadcasted_iota(jnp.int32, (LANES, LANES), 0)
    for s in range(row_count):
        hit = jnp.broadcast_to(high[s : s + 1], (high_count, LANES)) == high_iota
        left = [
            jnp.where(hit, jnp.broadcast_to(part[s : s + 1], (high_count, LANES)), 0.0).astype(jnp.bfloat16)
            for part in parts
        ]
        lefts.append(jnp.concatenate(left, axis=0))
        right = jnp.broadcast_to(low[s : s + 1], (LANES, LANES)) == low_iota
        rights.append(jnp.where(right, 1.0, 0.0).astype(jnp.bfloat16))
    left = jnp.concatenate(lefts, axis=1)
    right = jnp.concatenate(rights, axis=1)
    out = lax.dot_general(left, right, (((1,), (1,)), ((), ())), preferred_element_type=F32)
    sums = []
    for i in range(len(values)):
        base = 2 * i * high_count
        sums.append(out[base : base + high_count] + out[base + high_count : base + 2 * high_count])
    return sums


def pack_edges(rows):
    lane = lax.broadcasted_iota(jnp.int32, rows[0].shape, 1)
    half = LANES // 2
    packed = jnp.zeros(rows[0].shape, F32)
    for x, row in enumerate(rows):
        left = pltpu.roll(row, (x * HALO) % LANES, axis=1)
        right = pltpu.roll(row, (half + x * HALO + HALO) % LANES, axis=1)
        packed = jnp.where((lane >= x * HALO) & (lane < x * HALO + HALO), left, packed)
        base = half + x * HALO
        packed = jnp.where((lane >= base) & (lane < base + HALO), right, packed)
    return packed


def local_kernel(
    levels_all, rows_x,
    count_ref, state_ref, cell_ref, list_ref, gas_ref, source_ref,
    ghost_ref, bins_ref, field_ref, src_ref,
):
    groups = state_ref.shape[1] // LANES
    index = list_ref[...]
    picked = take_groups(
        lambda r, g: state_ref[r : r + 1, pl.ds(pl.multiple_of(g * LANES, LANES), LANES)],
        range(8), groups, [index >> 7], [index & 127], 4,
    )[0]
    lines = index.shape[0] // 4
    row_iota = lax.broadcasted_iota(jnp.int32, index.shape, 0)
    place = (row_iota % lines) * LANES + lax.broadcasted_iota(jnp.int32, index.shape, 1)
    quad = row_iota // lines
    limit = jnp.zeros(index.shape, jnp.int32)
    for q in range(4):
        limit = jnp.where(quad == q, count_ref[q], limit)
    live = place < limit
    width = lines * LANES
    for r in range(8):
        value = jnp.where(live, picked[r], FAR if r < 3 else 0.0)
        for s, (a, b) in enumerate(SLOTS):
            q = ((a + 1) % 2) * 2 + (b + 1) % 2
            shift = SHIFTS[a] if r == 0 else SHIFTS[b] if r == 1 else 0
            for line in range(lines):
                row = value[q * lines + line : q * lines + line + 1]
                if r < 2:
                    row = row + float(shift)
                base = s * width + line * LANES
                ghost_ref[r : r + 1, base : base + LANES] = row

    high_count = rows_x * levels_all
    totals = None
    for block in range(groups // SUB):
        rows = [
            jnp.concatenate(
                [
                    state_ref[r : r + 1, (block * SUB + s) * LANES : (block * SUB + s + 1) * LANES]
                    for s in range(SUB)
                ],
                axis=0,
            )
            for r in (3, 4, 5, 6)
        ]
        radius = rows[3]
        drag = BETA_RATE * radius
        values = [VOLUME * radius * radius * radius, drag] + [drag * rows[c] for c in range(3)]
        cell = cell_ref[block * SUB : (block + 1) * SUB, :]
        line = cell >> 7
        high = (line % rows_x) * levels_all + line // rows_x
        sums = spread_dot(values, high, cell & 127, high_count)
        totals = sums if totals is None else [t + s for t, s in zip(totals, sums)]
    for p in range(5):
        bins_ref[p] = totals[p].reshape(rows_x, levels_all, LANES)
    for c in range(3):
        for x in range(rows_x):
            field_ref[c, x] = gas_ref[c, :, x, :]
            src_ref[c, x] = source_ref[c, :, x, :]


def exchange_kernel(
    sizes,
    state_ref, ghost_ref, bins_ref, field_ref, src_ref,
    tile_ref, gas_ref, block_ref,
    bins_in, edges, above, below, send_sem, recv_sem,
):
    n_x, n_y, n_h = sizes
    x, y, h = (lax.axis_index(name) for name in ("tx", "ty", "solver"))
    levels = field_ref.shape[2]
    rows_x = field_ref.shape[1]
    own = state_ref.shape[1]
    barrier = pltpu.get_barrier_semaphore()
    up = (y + 1) % n_y
    down = (y + n_y - 1) % n_y
    partner = (h + 1) % n_h
    for dx in (0, 1, n_x - 1):
        for line in (y, up, down):
            for k in range(n_h):
                if dx or k or line is not y:
                    target = ((x + dx) % n_x, line, (h + k) % n_h)
                    pl.semaphore_signal(barrier, inc=1, device_id=target, device_id_type=MESH)
    pl.semaphore_wait(barrier, 9 * n_h - 1)

    copies = []

    def send(src, dst, kind, target):
        copy = pltpu.make_async_remote_copy(
            src_ref=src, dst_ref=dst, send_sem=send_sem.at[len(copies)], recv_sem=recv_sem.at[kind],
            device_id=target, device_id_type=MESH,
        )
        copy.start()
        copies.append(copy)

    theirs = pl.multiple_of(partner * levels, levels)
    here = pl.multiple_of(h * levels, levels)
    send(bins_ref.at[:, :, pl.ds(theirs, levels), :], bins_in, 0, (x, y, partner))
    cycle = ghost_ref.shape[1]
    width = cycle // len(SLOTS)
    base = n_h * own + h * cycle
    runs = ((0, 1), (1, 2), (3, 1), (4, 1), (5, 1), (6, 1), (7, 1), (8, 1), (9, 2), (11, 1))
    for first, length in runs:
        a, b = SLOTS[first]
        to_x = (x + n_x - SHIFTS[a]) % n_x
        to_y = (y + n_y - SHIFTS[b]) % n_y
        src = ghost_ref.at[:, first * width : (first + length) * width]
        dst = tile_ref.at[:, pl.ds(pl.multiple_of(base + first * width, width), length * width)]
        for k in range(n_h):
            send(src, dst, 1, (to_x, to_y, (h + k) % n_h))
    state_at = tile_ref.at[:, pl.ds(pl.multiple_of(h * own, own), own)]
    send(state_ref, state_at, 1, (x, y, partner))
    pltpu.make_async_copy(state_ref, state_at, recv_sem.at[1]).start()
    gas_at = gas_ref.at[:, :, pl.ds(here, levels), :]
    send(field_ref, gas_at, 2, (x, y, partner))
    pltpu.make_async_copy(field_ref, gas_at, recv_sem.at[2]).start()

    pltpu.make_async_copy(bins_in, bins_in, recv_sem.at[0]).wait()
    edge_rows = [[] for _ in range(7)]
    for i in range(rows_x):
        sums = [bins_ref[p, i, pl.ds(here, levels), :] + bins_in[p, i] for p in range(5)]
        porous = 1.0 / (1.0 + sums[0])
        inverse = 1.0 / (porous + sums[1] + 6.0 * VISCOSITY)
        gas = [field_ref[c, i] for c in range(3)]
        values = [porous * gas[c] + sums[2 + c] + src_ref[c, i] for c in range(3)] + [inverse] + gas
        for p in range(7):
            block_ref[p, i] = values[p]
            edge_rows[p].append(values[p])
    for p in range(7):
        edges[p] = pack_edges(edge_rows[p])
    send(edges, above, 3, (x, down, h))
    send(edges, below, 4, (x, up, h))
    pltpu.make_async_copy(above, above, recv_sem.at[3]).wait()
    pltpu.make_async_copy(below, below, recv_sem.at[4]).wait()
    lane = lax.broadcasted_iota(jnp.int32, (levels, LANES), 1)
    for p in range(7):
        block_ref[p, rows_x] = jnp.where(lane < LANES // 2, above[p], below[p])
    for kind, ref in ((1, tile_ref), (2, gas_ref)):
        pltpu.make_async_copy(ref, ref, recv_sem.at[kind]).wait()
    for copy in copies:
        copy.wait_send()


def load_table(target, load_row, rows, groups):
    @pl.loop(0, groups // 16)
    def _(step):
        for r in range(rows):
            lines = [load_row(r, step * 16 + j) for j in range(16)]
            value = jnp.concatenate(lines, axis=0)
            high = value.astype(jnp.bfloat16)
            at = pl.ds(pl.multiple_of(r * groups + step * 16, 16), 16)
            target[at, 0:LANES] = high
            target[at, LANES : 2 * LANES] = (value - high.astype(F32)).astype(jnp.bfloat16)


def pick(table, rows, groups, index, target):
    n = 2
    for q in range(SUB // n):
        line = jnp.concatenate([index[q * n + i : q * n + i + 1] for i in range(n)], axis=1)
        shape = (LANES, n * LANES)
        hot = jnp.broadcast_to(line & (LANES - 1), shape) == lax.broadcasted_iota(jnp.int32, shape, 0)
        hot = jnp.where(hot, 1.0, 0.0).astype(jnp.bfloat16)
        hot = jnp.concatenate([hot, hot], axis=0)
        shape = (groups, n * LANES)
        hit = jnp.broadcast_to(line >> 7, shape) == lax.broadcasted_iota(jnp.int32, shape, 0)
        full = jnp.dot(table[...], hot, preferred_element_type=F32)
        for r in range(rows):
            part = jnp.where(hit, full[r * groups : (r + 1) * groups], 0.0)
            part = jnp.sum(part, axis=0, keepdims=True)
            for i in range(n):
                target[r, q * n + i : q * n + i + 1, :] = part[:, i * LANES : (i + 1) * LANES]


def pair_kernel(
    rows_x,
    count_ref, tile_ref, state_ref, state_rows, cell_ref, own_ref, other_ref, gas_ref,
    out_ref, force_ref, own_table, tile_table, gas_table, first_ref, second_ref,
):
    levels_all = gas_ref.shape[2]
    groups = state_ref.shape[1] // LANES
    tile_groups = tile_ref.shape[1] // LANES
    load_table(
        own_table, lambda r, g: state_ref[r : r + 1, pl.ds(pl.multiple_of(g * LANES, LANES), LANES)], 7, groups
    )
    load_table(
        tile_table, lambda r, g: tile_ref[r : r + 1, pl.ds(pl.multiple_of(g * LANES, LANES), LANES)], 7, tile_groups
    )
    load_table(
        gas_table, lambda c, g: gas_ref[c, g // levels_all, pl.ds(g % levels_all, 1), :], 3, rows_x * levels_all
    )
    force_ref[...] = jnp.zeros_like(force_ref)
    count = count_ref[0]
    block = SUB * LANES

    @pl.loop(0, (count + block - 1) // block)
    def _(round_index):
        start = pl.multiple_of(round_index * SUB, SUB)
        own = own_ref[pl.ds(start, SUB), :]
        pick(own_table, 7, groups, own, first_ref)
        pick(tile_table, 7, tile_groups, other_ref[pl.ds(start, SUB), :], second_ref)
        a = [first_ref[r] for r in range(7)]
        b = [second_ref[r] for r in range(7)]
        gap = [a[c] - b[c] for c in range(3)]
        distance = jnp.sqrt(gap[0] * gap[0] + gap[1] * gap[1] + gap[2] * gap[2])
        scale = 1.0 / jnp.maximum(distance, FLOOR)
        normal = [v * scale for v in gap]
        overlap = jnp.maximum(a[6] + b[6] - distance, 0.0)
        closing = sum((a[3 + c] - b[3 + c]) * normal[c] for c in range(3))
        root = jnp.sqrt(overlap)
        size = STIFF * overlap * root - DAMPING * root * closing
        place = (start + lax.broadcasted_iota(jnp.int32, (SUB, LANES), 0)) * LANES
        place = place + lax.broadcasted_iota(jnp.int32, (SUB, LANES), 1)
        size = jnp.where(place < count, size, 0.0)
        sums = spread_dot([size * v for v in normal], own >> 7, own & 127, groups)
        for c in range(3):
            force_ref[c] += sums[c]

    @pl.loop(0, groups // SUB)
    def _(i):
        span = pl.ds(pl.multiple_of(i * SUB, SUB), SUB)
        cell = cell_ref[span, :]
        line = cell >> 7
        high = (line % rows_x) * levels_all + line // rows_x
        pick(gas_table, 3, rows_x * levels_all, high * LANES + (cell & 127), first_ref)
        drag = BETA_RATE * state_rows[6, span, :]
        rate = TIME_STEP / state_rows[7, span, :]
        for c in range(3):
            velocity = state_rows[3 + c, span, :]
            value = velocity + (force_ref[c, span, :] + drag * (first_ref[c] - velocity)) * rate
            if c == 2:
                value = value - TIME_STEP * GRAVITY
            out_ref[c, span, :] = value


def sweep_kernel(rows_x, n_h, whole, out_ref, field_a, field_b, rhs_ref):
    n_all, levels_all = field_a.shape[1:3]
    levels = out_ref.shape[1]
    x, h = lax.axis_index("tx"), lax.axis_index("solver")
    lane = lax.broadcasted_iota(jnp.int32, (levels, LANES), 1)

    @pl.loop(0, n_all // rows_x)
    def _(t):
        for k in range(n_h):
            span = slice(k * levels, (k + 1) * levels)
            for p in range(7):
                target, q = (rhs_ref, p) if p < 4 else (field_a, p - 4)
                edge_row = whole[t * n_h + k, p, rows_x]
                for i in range(rows_x):
                    at = t * rows_x + i
                    target[q, at, span, 0:LANES] = whole[t * n_h + k, p, i]
                    right = pltpu.roll(edge_row, (LANES - i * HALO) % LANES, axis=1)
                    left = pltpu.roll(edge_row, (LANES // 2 - (i + 1) * HALO) % LANES, axis=1)
                    edge = jnp.where(lane < HALO, right, jnp.where(lane >= LANES - HALO, left, 0.0))
                    target[q, at, span, LANES : 2 * LANES] = edge

    level = lax.broadcasted_iota(jnp.int32, (levels_all, 2 * LANES), 0)

    def sweep(source, target):
        @pl.loop(0, n_all // 2)
        def _(pair):
            for j in range(2):
                at = pair * 2 + j
                inverse = rhs_ref[3, at]
                for c in range(3):
                    mid = source[c, at]
                    total = rhs_ref[c, at] + source[c, (at + 1) % n_all] + source[c, (at + n_all - 1) % n_all]
                    total = total + jnp.where(level == 0, 0.0, pltpu.roll(mid, 1, axis=0))
                    total = total + jnp.where(level == levels_all - 1, 0.0, pltpu.roll(mid, levels_all - 1, axis=0))
                    total = total + pltpu.roll(mid, 1, axis=1) + pltpu.roll(mid, 2 * LANES - 1, axis=1)
                    target[c, at] = total * inverse

    @pl.loop(0, ITERS // 2)
    def _(step):
        sweep(field_a, field_b)
        sweep(field_b, field_a)

    here = pl.multiple_of(h * levels, levels)
    for c in range(3):
        for i in range(rows_x):
            out_ref[c, :, i, :] = field_a[c, x * rows_x + i, pl.ds(here, levels), 0:LANES]


def on_device(
    sizes,
    particle_state, particle_cell, boundary_list, boundary_count,
    contact_own, contact_other, contact_count, gas_velocity, gas_source,
):
    n_x, n_y, n_h = sizes
    own = particle_state.shape[1]
    levels, rows_x, rows_y = gas_velocity.shape[1:]
    levels_all = levels * n_h
    width = boundary_list.shape[-1]
    cycle = len(SLOTS) * width
    shape = lambda *dims: jax.ShapeDtypeStruct(dims, F32)
    smem = pl.BlockSpec(memory_space=pltpu.SMEM)
    params = functools.partial(pltpu.CompilerParams, vmem_limit_bytes=VMEM_LIMIT)
    cells = particle_cell.reshape(-1, LANES)
    ghosts, bins, field, source = pl.pallas_call(
        functools.partial(local_kernel, levels_all, rows_x),
        out_shape=(
            shape(8, cycle), shape(5, rows_x, levels_all, rows_y), shape(3, rows_x, levels, rows_y),
            shape(3, rows_x, levels, rows_y),
        ),
        in_specs=[smem] + vmem_specs(5),
        out_specs=tuple(vmem_specs(4)),
        compiler_params=params(),
        name="local",
    )(
        boundary_count.reshape(4), particle_state, cells, boundary_list.reshape(-1, LANES),
        gas_velocity, gas_source,
    )
    n_all = n_x * rows_x
    sends = 5 + 10 * n_h
    tile, gas_own, block = pl.pallas_call(
        functools.partial(exchange_kernel, sizes),
        out_shape=(
            shape(8, n_h * (own + cycle)), shape(3, rows_x, levels_all, rows_y),
            shape(7, rows_x + 1, levels, rows_y),
        ),
        in_specs=vmem_specs(5),
        out_specs=tuple(vmem_specs(3)),
        scratch_shapes=[
            pltpu.VMEM((5, rows_x, levels, rows_y), F32),
            pltpu.VMEM((7, levels, LANES), F32),
            pltpu.VMEM((7, levels, LANES), F32),
            pltpu.VMEM((7, levels, LANES), F32),
            pltpu.SemaphoreType.DMA((sends,)),
            pltpu.SemaphoreType.DMA((5,)),
        ],
        compiler_params=params(collective_id=0, has_side_effects=True),
        name="exchange",
    )(particle_state, ghosts, bins, field, source)
    whole = lax.all_gather(block, ("tx", "solver"))
    tile_groups = tile.shape[1] // LANES
    moved = pl.pallas_call(
        functools.partial(pair_kernel, rows_x),
        out_shape=shape(3, own // LANES, LANES),
        in_specs=[smem] + vmem_specs(7),
        out_specs=vmem_specs(1)[0],
        scratch_shapes=[
            pltpu.VMEM((3, own // LANES, LANES), F32),
            pltpu.VMEM((7 * own // LANES, 2 * LANES), jnp.bfloat16),
            pltpu.VMEM((7 * tile_groups, 2 * LANES), jnp.bfloat16),
            pltpu.VMEM((3 * rows_x * levels_all, 2 * LANES), jnp.bfloat16),
            pltpu.VMEM((7, SUB, LANES), F32),
            pltpu.VMEM((7, SUB, LANES), F32),
        ],
        compiler_params=params(),
        cost_estimate=pl.CostEstimate(flops=10**10, bytes_accessed=10**8, transcendentals=0),
        name="pairs",
    )(
        contact_count.reshape(1), tile, particle_state, particle_state.reshape(8, -1, LANES), cells,
        contact_own.reshape(-1, LANES), contact_other.reshape(-1, LANES), gas_own,
    )
    swept = pl.pallas_call(
        functools.partial(sweep_kernel, rows_x, n_h),
        out_shape=shape(3, levels, rows_x, rows_y),
        in_specs=vmem_specs(1),
        out_specs=vmem_specs(1)[0],
        scratch_shapes=[
            pltpu.VMEM((3, n_all, levels_all, 2 * LANES), F32),
            pltpu.VMEM((3, n_all, levels_all, 2 * LANES), F32),
            pltpu.VMEM((4, n_all, levels_all, 2 * LANES), F32),
        ],
        compiler_params=params(),
        name="sweeps",
    )(whole)
    return (moved.reshape(3, own), swept)


def solution(mesh):
    sizes = (mesh.shape["tx"], mesh.shape["ty"], mesh.shape["solver"])
    in_specs = (
        P(None, ("tx", "ty", "solver")),
        P(("tx", "ty", "solver")),
        P("tx", "ty", "solver", None, None, None),
        P("tx", "ty", "solver", None, None),
        P("tx", "ty", "solver", None),
        P("tx", "ty", "solver", None),
        P("tx", "ty", "solver"),
        P(None, "solver", "tx", "ty"),
        P(None, "solver", "tx", "ty"),
    )
    out_specs = (P(None, ("tx", "ty", "solver")), P(None, "solver", "tx", "ty"))
    return jax.shard_map(
        functools.partial(on_device, sizes), mesh=mesh, in_specs=in_specs, out_specs=out_specs, check_vma=False
    )
```

```python
import functools

import jax
import jax.numpy as jnp
from jax import lax
from jax.experimental import pallas as pl
from jax.experimental.pallas import tpu as pltpu
from jax.sharding import PartitionSpec as P

ITERS = 16
FAR = 100.0
STIFF = 4.0
DAMPING = 1.0
FLOOR = 0.1
BETA_RATE = 2.0
VOLUME = 4.18879
TIME_STEP = 0.1
GRAVITY = 1.0
VISCOSITY = 1.0
SUB = 8
LANES = 128
HALO = 16
SHIFTS = (-1, 0, 0, 1)
SLOTS = tuple((a, b) for a in range(4) for b in range(4) if not (a in (1, 2) and b in (1, 2)))
VMEM_LIMIT = 48 << 20
MESH = pl.DeviceIdType.MESH
F32 = jnp.float32


def vmem_specs(count):
    return [pl.BlockSpec(memory_space=pltpu.VMEM)] * count


def lane_take(row, low):
    return jnp.take_along_axis(jnp.broadcast_to(row, low.shape), low, axis=1, mode="promise_in_bounds")


def take_groups(load_row, rows, groups, high, low, unroll):
    chunks = high[0].shape
    start = tuple(jnp.zeros(chunks, F32) for _ in range(len(high) * len(rows)))

    def step(group, acc):
        out = []
        table = [load_row(r, group) for r in rows]
        for i in range(len(high)):
            hit = high[i] == group
            for j in range(len(rows)):
                out.append(jnp.where(hit, lane_take(table[j], low[i]), acc[i * len(rows) + j]))
        return tuple(out)

    flat = lax.fori_loop(0, groups, step, start, unroll=unroll)
    return [flat[i * len(rows) : (i + 1) * len(rows)] for i in range(len(high))]


def two_parts(value):
    high = value.astype(jnp.bfloat16).astype(F32)
    return (high, value - high)


def spread_dot(values, high, low, high_count):
    row_count = high.shape[0]
    parts = []
    for value in values:
        parts.extend(two_parts(value))
    lefts = []
    rights = []
    high_iota = lax.broadcasted_iota(jnp.int32, (high_count, LANES), 0)
    low_iota = lax.broadcasted_iota(jnp.int32, (LANES, LANES), 0)
    for s in range(row_count):
        hit = jnp.broadcast_to(high[s : s + 1], (high_count, LANES)) == high_iota
        left = [
            jnp.where(hit, jnp.broadcast_to(part[s : s + 1], (high_count, LANES)), 0.0).astype(jnp.bfloat16)
            for part in parts
        ]
        lefts.append(jnp.concatenate(left, axis=0))
        right = jnp.broadcast_to(low[s : s + 1], (LANES, LANES)) == low_iota
        rights.append(jnp.where(right, 1.0, 0.0).astype(jnp.bfloat16))
    left = jnp.concatenate(lefts, axis=1)
    right = jnp.concatenate(rights, axis=1)
    out = lax.dot_general(left, right, (((1,), (1,)), ((), ())), preferred_element_type=F32)
    sums = []
    for i in range(len(values)):
        base = 2 * i * high_count
        sums.append(out[base : base + high_count] + out[base + high_count : base + 2 * high_count])
    return sums


def pack_edges(rows):
    lane = lax.broadcasted_iota(jnp.int32, rows[0].shape, 1)
    half = LANES // 2
    packed = jnp.zeros(rows[0].shape, F32)
    for x, row in enumerate(rows):
        left = pltpu.roll(row, (x * HALO) % LANES, axis=1)
        right = pltpu.roll(row, (half + x * HALO + HALO) % LANES, axis=1)
        packed = jnp.where((lane >= x * HALO) & (lane < x * HALO + HALO), left, packed)
        base = half + x * HALO
        packed = jnp.where((lane >= base) & (lane < base + HALO), right, packed)
    return packed


def local_kernel(
    levels_all, rows_x,
    count_ref, state_ref, cell_ref, list_ref, gas_ref, source_ref,
    ghost_ref, bins_ref, field_ref, src_ref,
):
    groups = state_ref.shape[1] // LANES
    index = list_ref[...]
    picked = take_groups(
        lambda r, g: state_ref[r : r + 1, pl.ds(pl.multiple_of(g * LANES, LANES), LANES)],
        range(8), groups, [index >> 7], [index & 127], 4,
    )[0]
    lines = index.shape[0] // 4
    row_iota = lax.broadcasted_iota(jnp.int32, index.shape, 0)
    place = (row_iota % lines) * LANES + lax.broadcasted_iota(jnp.int32, index.shape, 1)
    quad = row_iota // lines
    limit = jnp.zeros(index.shape, jnp.int32)
    for q in range(4):
        limit = jnp.where(quad == q, count_ref[q], limit)
    live = place < limit
    width = lines * LANES
    for r in range(8):
        value = jnp.where(live, picked[r], FAR if r < 3 else 0.0)
        for s, (a, b) in enumerate(SLOTS):
            q = ((a + 1) % 2) * 2 + (b + 1) % 2
            shift = SHIFTS[a] if r == 0 else SHIFTS[b] if r == 1 else 0
            for line in range(lines):
                row = value[q * lines + line : q * lines + line + 1]
                if r < 2:
                    row = row + float(shift)
                base = s * width + line * LANES
                ghost_ref[r : r + 1, base : base + LANES] = row

    high_count = rows_x * levels_all
    totals = None
    for block in range(groups // SUB):
        rows = [
            jnp.concatenate(
                [
                    state_ref[r : r + 1, (block * SUB + s) * LANES : (block * SUB + s + 1) * LANES]
                    for s in range(SUB)
                ],
                axis=0,
            )
            for r in (3, 4, 5, 6)
        ]
        radius = rows[3]
        drag = BETA_RATE * radius
        values = [VOLUME * radius * radius * radius, drag] + [drag * rows[c] for c in range(3)]
        cell = cell_ref[block * SUB : (block + 1) * SUB, :]
        line = cell >> 7
        high = (line % rows_x) * levels_all + line // rows_x
        sums = spread_dot(values, high, cell & 127, high_count)
        totals = sums if totals is None else [t + s for t, s in zip(totals, sums)]
    for p in range(5):
        bins_ref[p] = totals[p].reshape(rows_x, levels_all, LANES)
    for c in range(3):
        for x in range(rows_x):
            field_ref[c, x] = gas_ref[c, :, x, :]
            src_ref[c, x] = source_ref[c, :, x, :]


def exchange_kernel(
    sizes,
    state_ref, ghost_ref, bins_ref, field_ref, src_ref,
    tile_ref, block_ref,
    bins_in, edges, above, below, send_sem, recv_sem,
):
    n_x, n_y, n_h = sizes
    x, y, h = (lax.axis_index(name) for name in ("tx", "ty", "solver"))
    levels = field_ref.shape[2]
    rows_x = field_ref.shape[1]
    own = state_ref.shape[1]
    barrier = pltpu.get_barrier_semaphore()
    up = (y + 1) % n_y
    down = (y + n_y - 1) % n_y
    partner = (h + 1) % n_h
    for dx in (0, 1, n_x - 1):
        for line in (y, up, down):
            for k in range(n_h):
                if dx or k or line is not y:
                    target = ((x + dx) % n_x, line, (h + k) % n_h)
                    pl.semaphore_signal(barrier, inc=1, device_id=target, device_id_type=MESH)
    pl.semaphore_wait(barrier, 9 * n_h - 1)

    copies = []

    def send(src, dst, kind, target):
        copy = pltpu.make_async_remote_copy(
            src_ref=src, dst_ref=dst, send_sem=send_sem.at[len(copies)], recv_sem=recv_sem.at[kind],
            device_id=target, device_id_type=MESH,
        )
        copy.start()
        copies.append(copy)

    theirs = pl.multiple_of(partner * levels, levels)
    here = pl.multiple_of(h * levels, levels)
    send(bins_ref.at[:, :, pl.ds(theirs, levels), :], bins_in, 0, (x, y, partner))
    cycle = ghost_ref.shape[1]
    width = cycle // len(SLOTS)
    base = n_h * own + h * cycle
    runs = ((0, 1), (1, 2), (3, 1), (4, 1), (5, 1), (6, 1), (7, 1), (8, 1), (9, 2), (11, 1))
    for first, length in runs:
        a, b = SLOTS[first]
        to_x = (x + n_x - SHIFTS[a]) % n_x
        to_y = (y + n_y - SHIFTS[b]) % n_y
        src = ghost_ref.at[:, first * width : (first + length) * width]
        dst = tile_ref.at[:, pl.ds(pl.multiple_of(base + first * width, width), length * width)]
        for k in range(n_h):
            send(src, dst, 1, (to_x, to_y, (h + k) % n_h))
    state_at = tile_ref.at[:, pl.ds(pl.multiple_of(h * own, own), own)]
    send(state_ref, state_at, 1, (x, y, partner))
    pltpu.make_async_copy(state_ref, state_at, recv_sem.at[1]).start()

    pltpu.make_async_copy(bins_in, bins_in, recv_sem.at[0]).wait()
    edge_rows = [[] for _ in range(7)]
    for i in range(rows_x):
        sums = [bins_ref[p, i, pl.ds(here, levels), :] + bins_in[p, i] for p in range(5)]
        porous = 1.0 / (1.0 + sums[0])
        inverse = 1.0 / (porous + sums[1] + 6.0 * VISCOSITY)
        gas = [field_ref[c, i] for c in range(3)]
        values = [porous * gas[c] + sums[2 + c] + src_ref[c, i] for c in range(3)] + [inverse] + gas
        for p in range(7):
            block_ref[p, i, pl.ds(here, levels), :] = values[p]
            edge_rows[p].append(values[p])
    for p in range(7):
        edges[p] = pack_edges(edge_rows[p])
    inner_at = block_ref.at[:, 0:rows_x, pl.ds(here, levels), :]
    send(edges, above, 3, (x, down, h))
    send(edges, below, 4, (x, up, h))
    send(inner_at, inner_at, 2, (x, y, partner))
    pltpu.make_async_copy(above, above, recv_sem.at[3]).wait()
    pltpu.make_async_copy(below, below, recv_sem.at[4]).wait()
    lane = lax.broadcasted_iota(jnp.int32, (levels, LANES), 1)
    for p in range(7):
        block_ref[p, rows_x, pl.ds(here, levels), :] = jnp.where(lane < LANES // 2, above[p], below[p])
    edge_at = block_ref.at[:, rows_x, pl.ds(here, levels), :]
    send(edge_at, edge_at, 5, (x, y, partner))
    for kind, ref in ((1, tile_ref), (2, inner_at), (5, edge_at)):
        pltpu.make_async_copy(ref, ref, recv_sem.at[kind]).wait()
    for copy in copies:
        copy.wait_send()


def load_table(target, load_row, rows, groups):
    @pl.loop(0, groups // 16)
    def _(step):
        for r in range(rows):
            lines = [load_row(r, step * 16 + j) for j in range(16)]
            value = jnp.concatenate(lines, axis=0)
            high = value.astype(jnp.bfloat16)
            at = pl.ds(pl.multiple_of(r * groups + step * 16, 16), 16)
            target[at, 0:LANES] = high
            target[at, LANES : 2 * LANES] = (value - high.astype(F32)).astype(jnp.bfloat16)


def pick(table, rows, groups, index, target):
    n = 2
    for q in range(SUB // n):
        line = jnp.concatenate([index[q * n + i : q * n + i + 1] for i in range(n)], axis=1)
        shape = (LANES, n * LANES)
        hot = jnp.broadcast_to(line & (LANES - 1), shape) == lax.broadcasted_iota(jnp.int32, shape, 0)
        hot = jnp.where(hot, 1.0, 0.0).astype(jnp.bfloat16)
        hot = jnp.concatenate([hot, hot], axis=0)
        shape = (groups, n * LANES)
        hit = jnp.broadcast_to(line >> 7, shape) == lax.broadcasted_iota(jnp.int32, shape, 0)
        full = jnp.dot(table[...], hot, preferred_element_type=F32)
        for r in range(rows):
            part = jnp.where(hit, full[r * groups : (r + 1) * groups], 0.0)
            part = jnp.sum(part, axis=0, keepdims=True)
            for i in range(n):
                target[r, q * n + i : q * n + i + 1, :] = part[:, i * LANES : (i + 1) * LANES]


def pair_kernel(
    rows_x,
    count_ref, tile_ref, state_ref, state_rows, cell_ref, own_ref, other_ref, gas_ref,
    out_ref, force_ref, own_table, tile_table, gas_table, first_ref, second_ref,
):
    levels_all = gas_ref.shape[2]
    groups = state_ref.shape[1] // LANES
    tile_groups = tile_ref.shape[1] // LANES
    load_table(
        own_table, lambda r, g: state_ref[r : r + 1, pl.ds(pl.multiple_of(g * LANES, LANES), LANES)], 7, groups
    )
    load_table(
        tile_table, lambda r, g: tile_ref[r : r + 1, pl.ds(pl.multiple_of(g * LANES, LANES), LANES)], 7, tile_groups
    )
    load_table(
        gas_table, lambda c, g: gas_ref[4 + c, g // levels_all, pl.ds(g % levels_all, 1), :], 3, rows_x * levels_all
    )
    force_ref[...] = jnp.zeros_like(force_ref)
    count = count_ref[0]
    block = SUB * LANES

    @pl.loop(0, (count + block - 1) // block)
    def _(round_index):
        start = pl.multiple_of(round_index * SUB, SUB)
        own = own_ref[pl.ds(start, SUB), :]
        pick(own_table, 7, groups, own, first_ref)
        pick(tile_table, 7, tile_groups, other_ref[pl.ds(start, SUB), :], second_ref)
        a = [first_ref[r] for r in range(7)]
        b = [second_ref[r] for r in range(7)]
        gap = [a[c] - b[c] for c in range(3)]
        distance = jnp.sqrt(gap[0] * gap[0] + gap[1] * gap[1] + gap[2] * gap[2])
        scale = 1.0 / jnp.maximum(distance, FLOOR)
        normal = [v * scale for v in gap]
        overlap = jnp.maximum(a[6] + b[6] - distance, 0.0)
        closing = sum((a[3 + c] - b[3 + c]) * normal[c] for c in range(3))
        root = jnp.sqrt(overlap)
        size = STIFF * overlap * root - DAMPING * root * closing
        place = (start + lax.broadcasted_iota(jnp.int32, (SUB, LANES), 0)) * LANES
        place = place + lax.broadcasted_iota(jnp.int32, (SUB, LANES), 1)
        size = jnp.where(place < count, size, 0.0)
        sums = spread_dot([size * v for v in normal], own >> 7, own & 127, groups)
        for c in range(3):
            force_ref[c] += sums[c]

    @pl.loop(0, groups // SUB)
    def _(i):
        span = pl.ds(pl.multiple_of(i * SUB, SUB), SUB)
        cell = cell_ref[span, :]
        line = cell >> 7
        high = (line % rows_x) * levels_all + line // rows_x
        pick(gas_table, 3, rows_x * levels_all, high * LANES + (cell & 127), first_ref)
        drag = BETA_RATE * state_rows[6, span, :]
        rate = TIME_STEP / state_rows[7, span, :]
        for c in range(3):
            velocity = state_rows[3 + c, span, :]
            value = velocity + (force_ref[c, span, :] + drag * (first_ref[c] - velocity)) * rate
            if c == 2:
                value = value - TIME_STEP * GRAVITY
            out_ref[c, span, :] = value


def sweep_kernel(rows_x, n_x, *refs):
    blocks, (mine_ref, theirs_ref, field_a, field_b, rhs_ref) = refs[:n_x], refs[n_x:]
    n_all, levels_all = field_a.shape[1:3]
    levels = mine_ref.shape[1]
    x, h = lax.axis_index("tx"), lax.axis_index("solver")
    lane = lax.broadcasted_iota(jnp.int32, (levels_all, LANES), 1)
    half = LANES // 2
    first = h * (half - HALO)
    kept = (lane >= first) & (lane < first + half + HALO)
    for step, whole in enumerate(blocks):
        t = (x + n_x - step) % n_x
        for p in range(7):
            target, q = (rhs_ref, p) if p < 4 else (field_a, p - 4)
            edge_row = whole[p, rows_x]
            for i in range(rows_x):
                right = pltpu.roll(edge_row, (LANES - i * HALO) % LANES, axis=1)
                left = pltpu.roll(edge_row, (half - (i + 1) * HALO) % LANES, axis=1)
                edge = jnp.where(lane < HALO, right, jnp.where(lane >= LANES - HALO, left, 0.0))
                target[q, t * rows_x + i] = jnp.where(kept, whole[p, i], edge)

    level = lax.broadcasted_iota(jnp.int32, (levels_all, LANES), 0)

    def sweep(source, target):
        @pl.loop(0, n_all // 2)
        def _(pair):
            for j in range(2):
                at = pair * 2 + j
                inverse = rhs_ref[3, at]
                for c in range(3):
                    mid = source[c, at]
                    total = rhs_ref[c, at] + source[c, (at + 1) % n_all] + source[c, (at + n_all - 1) % n_all]
                    total = total + jnp.where(level == 0, 0.0, pltpu.roll(mid, 1, axis=0))
                    total = total + jnp.where(level == levels_all - 1, 0.0, pltpu.roll(mid, levels_all - 1, axis=0))
                    total = total + pltpu.roll(mid, 1, axis=1) + pltpu.roll(mid, LANES - 1, axis=1)
                    target[c, at] = total * inverse

    @pl.loop(0, ITERS // 2)
    def _(step):
        sweep(field_a, field_b)
        sweep(field_b, field_a)

    here = pl.multiple_of(h * levels, levels)
    there = pl.multiple_of((1 - h) * levels, levels)
    for c in range(3):
        for i in range(rows_x):
            mine_ref[c, :, i, :] = field_a[c, x * rows_x + i, pl.ds(here, levels), :]
            theirs_ref[c, :, i, :] = field_a[c, x * rows_x + i, pl.ds(there, levels), :]


def on_device(
    sizes,
    particle_state, particle_cell, boundary_list, boundary_count,
    contact_own, contact_other, contact_count, gas_velocity, gas_source,
):
    n_x, n_y, n_h = sizes
    own = particle_state.shape[1]
    levels, rows_x, rows_y = gas_velocity.shape[1:]
    levels_all = levels * n_h
    width = boundary_list.shape[-1]
    cycle = len(SLOTS) * width
    shape = lambda *dims: jax.ShapeDtypeStruct(dims, F32)
    smem = pl.BlockSpec(memory_space=pltpu.SMEM)
    params = functools.partial(pltpu.CompilerParams, vmem_limit_bytes=VMEM_LIMIT)
    cells = particle_cell.reshape(-1, LANES)
    ghosts, bins, field, source = pl.pallas_call(
        functools.partial(local_kernel, levels_all, rows_x),
        out_shape=(
            shape(8, cycle), shape(5, rows_x, levels_all, rows_y), shape(3, rows_x, levels, rows_y),
            shape(3, rows_x, levels, rows_y),
        ),
        in_specs=[smem] + vmem_specs(5),
        out_specs=tuple(vmem_specs(4)),
        compiler_params=params(),
        name="local",
    )(
        boundary_count.reshape(4), particle_state, cells, boundary_list.reshape(-1, LANES),
        gas_velocity, gas_source,
    )
    n_all = n_x * rows_x
    sends = 6 + 10 * n_h
    tile, block = pl.pallas_call(
        functools.partial(exchange_kernel, sizes),
        out_shape=(
            shape(8, n_h * (own + cycle)), shape(7, rows_x + 1, levels_all, rows_y),
        ),
        in_specs=vmem_specs(5),
        out_specs=tuple(vmem_specs(2)),
        scratch_shapes=[
            pltpu.VMEM((5, rows_x, levels, rows_y), F32),
            pltpu.VMEM((7, levels, LANES), F32),
            pltpu.VMEM((7, levels, LANES), F32),
            pltpu.VMEM((7, levels, LANES), F32),
            pltpu.SemaphoreType.DMA((sends,)),
            pltpu.SemaphoreType.DMA((6,)),
        ],
        compiler_params=params(collective_id=0, has_side_effects=True),
        name="exchange",
    )(particle_state, ghosts, bins, field, source)
    blocks = [block] + [
        lax.ppermute(block, "tx", [(i, (i + step) % n_x) for i in range(n_x)]) for step in range(1, n_x)
    ]
    tile_groups = tile.shape[1] // LANES
    moved = pl.pallas_call(
        functools.partial(pair_kernel, rows_x),
        out_shape=shape(3, own // LANES, LANES),
        in_specs=[smem] + vmem_specs(7),
        out_specs=vmem_specs(1)[0],
        scratch_shapes=[
            pltpu.VMEM((3, own // LANES, LANES), F32),
            pltpu.VMEM((7 * own // LANES, 2 * LANES), jnp.bfloat16),
            pltpu.VMEM((7 * tile_groups, 2 * LANES), jnp.bfloat16),
            pltpu.VMEM((3 * rows_x * levels_all, 2 * LANES), jnp.bfloat16),
            pltpu.VMEM((7, SUB, LANES), F32),
            pltpu.VMEM((7, SUB, LANES), F32),
        ],
        compiler_params=params(),
        cost_estimate=pl.CostEstimate(flops=10**10, bytes_accessed=10**8, transcendentals=0),
        name="pairs",
    )(
        contact_count.reshape(1), tile, particle_state, particle_state.reshape(8, -1, LANES), cells,
        contact_own.reshape(-1, LANES), contact_other.reshape(-1, LANES), block,
    )
    mine, theirs = pl.pallas_call(
        functools.partial(sweep_kernel, rows_x, n_x),
        out_shape=(shape(3, levels, rows_x, rows_y), shape(3, levels, rows_x, rows_y)),
        in_specs=vmem_specs(n_x),
        out_specs=tuple(vmem_specs(2)),
        scratch_shapes=[
            pltpu.VMEM((3, n_all, levels_all, LANES), F32),
            pltpu.VMEM((3, n_all, levels_all, LANES), F32),
            pltpu.VMEM((4, n_all, levels_all, LANES), F32),
        ],
        compiler_params=params(),
        name="sweeps",
    )(*blocks)
    other_half = lax.ppermute(theirs, "solver", [(0, 1), (1, 0)])
    side = lax.broadcasted_iota(jnp.int32, mine.shape, 3) // (LANES // 2)
    swept = jnp.where(side == lax.axis_index("solver"), mine, other_half)
    return (moved.reshape(3, own), swept)


def solution(mesh):
    sizes = (mesh.shape["tx"], mesh.shape["ty"], mesh.shape["solver"])
    in_specs = (
        P(None, ("tx", "ty", "solver")),
        P(("tx", "ty", "solver")),
        P("tx", "ty", "solver", None, None, None),
        P("tx", "ty", "solver", None, None),
        P("tx", "ty", "solver", None),
        P("tx", "ty", "solver", None),
        P("tx", "ty", "solver"),
        P(None, "solver", "tx", "ty"),
        P(None, "solver", "tx", "ty"),
    )
    out_specs = (P(None, ("tx", "ty", "solver")), P(None, "solver", "tx", "ty"))
    return jax.shard_map(
        functools.partial(on_device, sizes), mesh=mesh, in_specs=in_specs, out_specs=out_specs, check_vma=False
    )
```

```python
import functools

import jax
import jax.numpy as jnp
from jax import lax
from jax.experimental import pallas as pl
from jax.experimental.pallas import tpu as pltpu
from jax.sharding import PartitionSpec as P

ITERS = 16
FAR = 100.0
STIFF = 4.0
DAMPING = 1.0
FLOOR = 0.1
BETA_RATE = 2.0
VOLUME = 4.18879
TIME_STEP = 0.1
GRAVITY = 1.0
VISCOSITY = 1.0
SUB = 8
LANES = 128
HALO = 16
SHIFTS = (-1, 0, 0, 1)
SLOTS = tuple((a, b) for a in range(4) for b in range(4) if not (a in (1, 2) and b in (1, 2)))
VMEM_LIMIT = 48 << 20
MESH = pl.DeviceIdType.MESH
F32 = jnp.float32


def vmem_specs(count):
    return [pl.BlockSpec(memory_space=pltpu.VMEM)] * count


def lane_take(row, low):
    return jnp.take_along_axis(jnp.broadcast_to(row, low.shape), low, axis=1, mode="promise_in_bounds")


def take_groups(load_row, rows, groups, high, low, unroll):
    chunks = high[0].shape
    start = tuple(jnp.zeros(chunks, F32) for _ in range(len(high) * len(rows)))

    def step(group, acc):
        out = []
        table = [load_row(r, group) for r in rows]
        for i in range(len(high)):
            hit = high[i] == group
            for j in range(len(rows)):
                out.append(jnp.where(hit, lane_take(table[j], low[i]), acc[i * len(rows) + j]))
        return tuple(out)

    flat = lax.fori_loop(0, groups, step, start, unroll=unroll)
    return [flat[i * len(rows) : (i + 1) * len(rows)] for i in range(len(high))]


def two_parts(value):
    high = value.astype(jnp.bfloat16).astype(F32)
    return (high, value - high)


def spread_dot(values, high, low, high_count):
    row_count = high.shape[0]
    parts = []
    for value in values:
        parts.extend(two_parts(value))
    lefts = []
    rights = []
    high_iota = lax.broadcasted_iota(jnp.int32, (high_count, LANES), 0)
    low_iota = lax.broadcasted_iota(jnp.int32, (LANES, LANES), 0)
    for s in range(row_count):
        hit = jnp.broadcast_to(high[s : s + 1], (high_count, LANES)) == high_iota
        left = [
            jnp.where(hit, jnp.broadcast_to(part[s : s + 1], (high_count, LANES)), 0.0).astype(jnp.bfloat16)
            for part in parts
        ]
        lefts.append(jnp.concatenate(left, axis=0))
        right = jnp.broadcast_to(low[s : s + 1], (LANES, LANES)) == low_iota
        rights.append(jnp.where(right, 1.0, 0.0).astype(jnp.bfloat16))
    left = jnp.concatenate(lefts, axis=1)
    right = jnp.concatenate(rights, axis=1)
    out = lax.dot_general(left, right, (((1,), (1,)), ((), ())), preferred_element_type=F32)
    sums = []
    for i in range(len(values)):
        base = 2 * i * high_count
        sums.append(out[base : base + high_count] + out[base + high_count : base + 2 * high_count])
    return sums


def pack_edges(rows):
    lane = lax.broadcasted_iota(jnp.int32, rows[0].shape, 1)
    half = LANES // 2
    packed = jnp.zeros(rows[0].shape, F32)
    for x, row in enumerate(rows):
        left = pltpu.roll(row, (x * HALO) % LANES, axis=1)
        right = pltpu.roll(row, (half + x * HALO + HALO) % LANES, axis=1)
        packed = jnp.where((lane >= x * HALO) & (lane < x * HALO + HALO), left, packed)
        base = half + x * HALO
        packed = jnp.where((lane >= base) & (lane < base + HALO), right, packed)
    return packed


def local_kernel(
    levels_all, rows_x,
    count_ref, state_ref, cell_ref, list_ref, gas_ref, source_ref,
    ghost_ref, bins_ref, field_ref, src_ref,
):
    groups = state_ref.shape[1] // LANES
    index = list_ref[...]
    picked = take_groups(
        lambda r, g: state_ref[r : r + 1, pl.ds(pl.multiple_of(g * LANES, LANES), LANES)],
        range(8), groups, [index >> 7], [index & 127], 4,
    )[0]
    lines = index.shape[0] // 4
    row_iota = lax.broadcasted_iota(jnp.int32, index.shape, 0)
    place = (row_iota % lines) * LANES + lax.broadcasted_iota(jnp.int32, index.shape, 1)
    quad = row_iota // lines
    limit = jnp.zeros(index.shape, jnp.int32)
    for q in range(4):
        limit = jnp.where(quad == q, count_ref[q], limit)
    live = place < limit
    width = lines * LANES
    for r in range(8):
        value = jnp.where(live, picked[r], FAR if r < 3 else 0.0)
        for s, (a, b) in enumerate(SLOTS):
            q = ((a + 1) % 2) * 2 + (b + 1) % 2
            shift = SHIFTS[a] if r == 0 else SHIFTS[b] if r == 1 else 0
            for line in range(lines):
                row = value[q * lines + line : q * lines + line + 1]
                if r < 2:
                    row = row + float(shift)
                base = s * width + line * LANES
                ghost_ref[r : r + 1, base : base + LANES] = row

    high_count = rows_x * levels_all
    totals = None
    for block in range(groups // SUB):
        rows = [
            jnp.concatenate(
                [
                    state_ref[r : r + 1, (block * SUB + s) * LANES : (block * SUB + s + 1) * LANES]
                    for s in range(SUB)
                ],
                axis=0,
            )
            for r in (3, 4, 5, 6)
        ]
        radius = rows[3]
        drag = BETA_RATE * radius
        values = [VOLUME * radius * radius * radius, drag] + [drag * rows[c] for c in range(3)]
        cell = cell_ref[block * SUB : (block + 1) * SUB, :]
        line = cell >> 7
        high = (line % rows_x) * levels_all + line // rows_x
        sums = spread_dot(values, high, cell & 127, high_count)
        totals = sums if totals is None else [t + s for t, s in zip(totals, sums)]
    for p in range(5):
        bins_ref[p] = totals[p].reshape(rows_x, levels_all, LANES)
    for c in range(3):
        for x in range(rows_x):
            field_ref[c, x] = gas_ref[c, :, x, :]
            src_ref[c, x] = source_ref[c, :, x, :]


def exchange_kernel(
    sizes,
    ghost_ref, bins_ref, field_ref, src_ref, other_gas,
    cycle_ref, block_ref,
    bins_in, edges, above, below, send_sem, recv_sem,
):
    n_x, n_y, n_h = sizes
    x, y, h = (lax.axis_index(name) for name in ("tx", "ty", "solver"))
    levels = field_ref.shape[2]
    rows_x = field_ref.shape[1]
    barrier = pltpu.get_barrier_semaphore()
    up = (y + 1) % n_y
    down = (y + n_y - 1) % n_y
    partner = (h + 1) % n_h
    for dx in (0, 1, n_x - 1):
        for line in (y, up, down):
            for k in range(n_h):
                if dx or k or line is not y:
                    target = ((x + dx) % n_x, line, (h + k) % n_h)
                    pl.semaphore_signal(barrier, inc=1, device_id=target, device_id_type=MESH)
    pl.semaphore_wait(barrier, 9 * n_h - 1)

    copies = []

    def send(src, dst, kind, target):
        copy = pltpu.make_async_remote_copy(
            src_ref=src, dst_ref=dst, send_sem=send_sem.at[len(copies)], recv_sem=recv_sem.at[kind],
            device_id=target, device_id_type=MESH,
        )
        copy.start()
        copies.append(copy)

    theirs = pl.multiple_of(partner * levels, levels)
    here = pl.multiple_of(h * levels, levels)
    send(bins_ref.at[:, :, pl.ds(theirs, levels), :], bins_in, 0, (x, y, partner))
    cycle = ghost_ref.shape[1]
    width = cycle // len(SLOTS)
    base = h * cycle
    runs = ((0, 1), (1, 2), (3, 1), (4, 1), (5, 1), (6, 1), (7, 1), (8, 1), (9, 2), (11, 1))
    for first, length in runs:
        a, b = SLOTS[first]
        to_x = (x + n_x - SHIFTS[a]) % n_x
        to_y = (y + n_y - SHIFTS[b]) % n_y
        src = ghost_ref.at[:, first * width : (first + length) * width]
        dst = cycle_ref.at[:, pl.ds(pl.multiple_of(base + first * width, width), length * width)]
        for k in range(n_h):
            send(src, dst, 1, (to_x, to_y, (h + k) % n_h))
    for c in range(3):
        for i in range(rows_x):
            block_ref[4 + c, i, pl.ds(theirs, levels), :] = other_gas[c, :, i, :]

    pltpu.make_async_copy(bins_in, bins_in, recv_sem.at[0]).wait()
    edge_rows = [[] for _ in range(7)]
    for i in range(rows_x):
        sums = [bins_ref[p, i, pl.ds(here, levels), :] + bins_in[p, i] for p in range(5)]
        porous = 1.0 / (1.0 + sums[0])
        inverse = 1.0 / (porous + sums[1] + 6.0 * VISCOSITY)
        gas = [field_ref[c, i] for c in range(3)]
        values = [porous * gas[c] + sums[2 + c] + src_ref[c, i] for c in range(3)] + [inverse] + gas
        for p in range(7):
            block_ref[p, i, pl.ds(here, levels), :] = values[p]
            edge_rows[p].append(values[p])
    for p in range(7):
        edges[p] = pack_edges(edge_rows[p])
    inner_at = block_ref.at[0:4, 0:rows_x, pl.ds(here, levels), :]
    send(edges, above, 3, (x, down, h))
    send(edges, below, 4, (x, up, h))
    send(inner_at, inner_at, 2, (x, y, partner))
    pltpu.make_async_copy(above, above, recv_sem.at[3]).wait()
    pltpu.make_async_copy(below, below, recv_sem.at[4]).wait()
    lane = lax.broadcasted_iota(jnp.int32, (levels, LANES), 1)
    for p in range(7):
        block_ref[p, rows_x, pl.ds(here, levels), :] = jnp.where(lane < LANES // 2, above[p], below[p])
    edge_at = block_ref.at[:, rows_x, pl.ds(here, levels), :]
    send(edge_at, edge_at, 5, (x, y, partner))
    for kind, ref in ((1, cycle_ref), (2, inner_at), (5, edge_at)):
        pltpu.make_async_copy(ref, ref, recv_sem.at[kind]).wait()
    for copy in copies:
        copy.wait_send()


def load_table(target, load_row, rows, groups, first, count):
    @pl.loop(0, count // 16)
    def _(step):
        for r in range(rows):
            lines = [load_row(r, step * 16 + j) for j in range(16)]
            value = jnp.concatenate(lines, axis=0)
            high = value.astype(jnp.bfloat16)
            at = pl.ds(pl.multiple_of(r * groups + first + step * 16, 16), 16)
            target[at, 0:LANES] = high
            target[at, LANES : 2 * LANES] = (value - high.astype(F32)).astype(jnp.bfloat16)


def pick(table, rows, groups, index, target):
    n = 2
    for q in range(SUB // n):
        line = jnp.concatenate([index[q * n + i : q * n + i + 1] for i in range(n)], axis=1)
        shape = (LANES, n * LANES)
        hot = jnp.broadcast_to(line & (LANES - 1), shape) == lax.broadcasted_iota(jnp.int32, shape, 0)
        hot = jnp.where(hot, 1.0, 0.0).astype(jnp.bfloat16)
        hot = jnp.concatenate([hot, hot], axis=0)
        shape = (groups, n * LANES)
        hit = jnp.broadcast_to(line >> 7, shape) == lax.broadcasted_iota(jnp.int32, shape, 0)
        full = jnp.dot(table[...], hot, preferred_element_type=F32)
        for r in range(rows):
            part = jnp.where(hit, full[r * groups : (r + 1) * groups], 0.0)
            part = jnp.sum(part, axis=0, keepdims=True)
            for i in range(n):
                target[r, q * n + i : q * n + i + 1, :] = part[:, i * LANES : (i + 1) * LANES]


def pair_kernel(
    rows_x,
    count_ref, cycle_ref, other_state, state_ref, state_rows, cell_ref, own_ref, other_ref, gas_ref,
    out_ref, force_ref, own_table, tile_table, gas_table, first_ref, second_ref,
):
    levels_all = gas_ref.shape[2]
    groups = state_ref.shape[1] // LANES
    cycle_groups = cycle_ref.shape[1] // LANES
    tile_groups = 2 * groups + cycle_groups
    h = lax.axis_index("solver")

    def columns(ref):
        return lambda r, g: ref[r : r + 1, pl.ds(pl.multiple_of(g * LANES, LANES), LANES)]

    load_table(own_table, columns(state_ref), 7, groups, 0, groups)
    load_table(tile_table, columns(state_ref), 7, tile_groups, h * groups, groups)
    load_table(tile_table, columns(other_state), 7, tile_groups, (1 - h) * groups, groups)
    load_table(tile_table, columns(cycle_ref), 7, tile_groups, 2 * groups, cycle_groups)
    load_table(
        gas_table, lambda c, g: gas_ref[4 + c, g // levels_all, pl.ds(g % levels_all, 1), :],
        3, rows_x * levels_all, 0, rows_x * levels_all,
    )
    force_ref[...] = jnp.zeros_like(force_ref)
    count = count_ref[0]
    block = SUB * LANES

    @pl.loop(0, (count + block - 1) // block)
    def _(round_index):
        start = pl.multiple_of(round_index * SUB, SUB)
        own = own_ref[pl.ds(start, SUB), :]
        pick(own_table, 7, groups, own, first_ref)
        pick(tile_table, 7, tile_groups, other_ref[pl.ds(start, SUB), :], second_ref)
        a = [first_ref[r] for r in range(7)]
        b = [second_ref[r] for r in range(7)]
        gap = [a[c] - b[c] for c in range(3)]
        distance = jnp.sqrt(gap[0] * gap[0] + gap[1] * gap[1] + gap[2] * gap[2])
        scale = 1.0 / jnp.maximum(distance, FLOOR)
        normal = [v * scale for v in gap]
        overlap = jnp.maximum(a[6] + b[6] - distance, 0.0)
        closing = sum((a[3 + c] - b[3 + c]) * normal[c] for c in range(3))
        root = jnp.sqrt(overlap)
        size = STIFF * overlap * root - DAMPING * root * closing
        place = (start + lax.broadcasted_iota(jnp.int32, (SUB, LANES), 0)) * LANES
        place = place + lax.broadcasted_iota(jnp.int32, (SUB, LANES), 1)
        size = jnp.where(place < count, size, 0.0)
        sums = spread_dot([size * v for v in normal], own >> 7, own & 127, groups)
        for c in range(3):
            force_ref[c] += sums[c]

    @pl.loop(0, groups // SUB)
    def _(i):
        span = pl.ds(pl.multiple_of(i * SUB, SUB), SUB)
        cell = cell_ref[span, :]
        line = cell >> 7
        high = (line % rows_x) * levels_all + line // rows_x
        pick(gas_table, 3, rows_x * levels_all, high * LANES + (cell & 127), first_ref)
        drag = BETA_RATE * state_rows[6, span, :]
        rate = TIME_STEP / state_rows[7, span, :]
        for c in range(3):
            velocity = state_rows[3 + c, span, :]
            value = velocity + (force_ref[c, span, :] + drag * (first_ref[c] - velocity)) * rate
            if c == 2:
                value = value - TIME_STEP * GRAVITY
            out_ref[c, span, :] = value


def sweep_kernel(rows_x, n_x, *refs):
    blocks, (mine_ref, theirs_ref, field_a, field_b, rhs_ref) = refs[:n_x], refs[n_x:]
    n_all, levels_all = field_a.shape[1:3]
    levels = mine_ref.shape[1]
    x, h = lax.axis_index("tx"), lax.axis_index("solver")
    lane = lax.broadcasted_iota(jnp.int32, (levels_all, LANES), 1)
    half = LANES // 2
    first = h * (half - HALO)
    kept = (lane >= first) & (lane < first + half + HALO)
    for step, whole in enumerate(blocks):
        t = (x + n_x - step) % n_x
        for p in range(7):
            target, q = (rhs_ref, p) if p < 4 else (field_a, p - 4)
            edge_row = whole[p, rows_x]
            for i in range(rows_x):
                right = pltpu.roll(edge_row, (LANES - i * HALO) % LANES, axis=1)
                left = pltpu.roll(edge_row, (half - (i + 1) * HALO) % LANES, axis=1)
                edge = jnp.where(lane < HALO, right, jnp.where(lane >= LANES - HALO, left, 0.0))
                target[q, t * rows_x + i] = jnp.where(kept, whole[p, i], edge)

    level = lax.broadcasted_iota(jnp.int32, (levels_all, LANES), 0)
    span = min(16, n_all)

    def sweep(source, target):
        @pl.loop(0, n_all // span)
        def _(part):
            for j in range(span):
                at = part * span + j
                inverse = rhs_ref[3, at]
                for c in range(3):
                    mid = source[c, at]
                    total = rhs_ref[c, at] + source[c, (at + 1) % n_all] + source[c, (at + n_all - 1) % n_all]
                    total = total + jnp.where(level == 0, 0.0, pltpu.roll(mid, 1, axis=0))
                    total = total + jnp.where(level == levels_all - 1, 0.0, pltpu.roll(mid, levels_all - 1, axis=0))
                    total = total + pltpu.roll(mid, 1, axis=1) + pltpu.roll(mid, LANES - 1, axis=1)
                    target[c, at] = total * inverse

    @pl.loop(0, ITERS // 2)
    def _(step):
        sweep(field_a, field_b)
        sweep(field_b, field_a)

    here = pl.multiple_of(h * levels, levels)
    there = pl.multiple_of((1 - h) * levels, levels)
    for c in range(3):
        for i in range(rows_x):
            mine_ref[c, :, i, :] = field_a[c, x * rows_x + i, pl.ds(here, levels), :]
            theirs_ref[c, :, i, :] = field_a[c, x * rows_x + i, pl.ds(there, levels), :]


def on_device(
    sizes,
    particle_state, particle_cell, boundary_list, boundary_count,
    contact_own, contact_other, contact_count, gas_velocity, gas_source,
):
    n_x, n_y, n_h = sizes
    own = particle_state.shape[1]
    levels, rows_x, rows_y = gas_velocity.shape[1:]
    levels_all = levels * n_h
    width = boundary_list.shape[-1]
    cycle = len(SLOTS) * width
    shape = lambda *dims: jax.ShapeDtypeStruct(dims, F32)
    smem = pl.BlockSpec(memory_space=pltpu.SMEM)
    params = functools.partial(pltpu.CompilerParams, vmem_limit_bytes=VMEM_LIMIT)
    cells = particle_cell.reshape(-1, LANES)
    swap = [(0, 1), (1, 0)]
    other_state = lax.ppermute(particle_state, "solver", swap)
    other_gas = lax.ppermute(gas_velocity, "solver", swap)
    ghosts, bins, field, source = pl.pallas_call(
        functools.partial(local_kernel, levels_all, rows_x),
        out_shape=(
            shape(8, cycle), shape(5, rows_x, levels_all, rows_y), shape(3, rows_x, levels, rows_y),
            shape(3, rows_x, levels, rows_y),
        ),
        in_specs=[smem] + vmem_specs(5),
        out_specs=tuple(vmem_specs(4)),
        compiler_params=params(),
        name="local",
    )(
        boundary_count.reshape(4), particle_state, cells, boundary_list.reshape(-1, LANES),
        gas_velocity, gas_source,
    )
    n_all = n_x * rows_x
    sends = 5 + 10 * n_h
    ghosts, other_state = lax.optimization_barrier((ghosts, other_state))
    cycles, block = pl.pallas_call(
        functools.partial(exchange_kernel, sizes),
        out_shape=(
            shape(8, n_h * cycle), shape(7, rows_x + 1, levels_all, rows_y),
        ),
        in_specs=vmem_specs(5),
        out_specs=tuple(vmem_specs(2)),
        scratch_shapes=[
            pltpu.VMEM((5, rows_x, levels, rows_y), F32),
            pltpu.VMEM((7, levels, LANES), F32),
            pltpu.VMEM((7, levels, LANES), F32),
            pltpu.VMEM((7, levels, LANES), F32),
            pltpu.SemaphoreType.DMA((sends,)),
            pltpu.SemaphoreType.DMA((6,)),
        ],
        compiler_params=params(collective_id=0, has_side_effects=True),
        name="exchange",
    )(ghosts, bins, field, source, other_gas)
    blocks = [block] + [
        lax.ppermute(block, "tx", [(i, (i + step) % n_x) for i in range(n_x)]) for step in range(1, n_x)
    ]
    tile_groups = n_h * (own + cycle) // LANES
    moved = pl.pallas_call(
        functools.partial(pair_kernel, rows_x),
        out_shape=shape(3, own // LANES, LANES),
        in_specs=[smem] + vmem_specs(8),
        out_specs=vmem_specs(1)[0],
        scratch_shapes=[
            pltpu.VMEM((3, own // LANES, LANES), F32),
            pltpu.VMEM((7 * own // LANES, 2 * LANES), jnp.bfloat16),
            pltpu.VMEM((7 * tile_groups, 2 * LANES), jnp.bfloat16),
            pltpu.VMEM((3 * rows_x * levels_all, 2 * LANES), jnp.bfloat16),
            pltpu.VMEM((7, SUB, LANES), F32),
            pltpu.VMEM((7, SUB, LANES), F32),
        ],
        compiler_params=params(),
        cost_estimate=pl.CostEstimate(flops=10**10, bytes_accessed=10**8, transcendentals=0),
        name="pairs",
    )(
        contact_count.reshape(1), cycles, other_state, particle_state, particle_state.reshape(8, -1, LANES), cells,
        contact_own.reshape(-1, LANES), contact_other.reshape(-1, LANES), block,
    )
    moved, blocks[0] = lax.optimization_barrier((moved, block))
    mine, theirs = pl.pallas_call(
        functools.partial(sweep_kernel, rows_x, n_x),
        out_shape=(shape(3, levels, rows_x, rows_y), shape(3, levels, rows_x, rows_y)),
        in_specs=vmem_specs(n_x),
        out_specs=tuple(vmem_specs(2)),
        scratch_shapes=[
            pltpu.VMEM((3, n_all, levels_all, LANES), F32),
            pltpu.VMEM((3, n_all, levels_all, LANES), F32),
            pltpu.VMEM((4, n_all, levels_all, LANES), F32),
        ],
        compiler_params=params(),
        name="sweeps",
    )(*blocks)
    other_half = lax.ppermute(theirs, "solver", swap)
    side = lax.broadcasted_iota(jnp.int32, mine.shape, 3) // (LANES // 2)
    swept = jnp.where(side == lax.axis_index("solver"), mine, other_half)
    return (moved.reshape(3, own), swept)


def solution(mesh):
    sizes = (mesh.shape["tx"], mesh.shape["ty"], mesh.shape["solver"])
    in_specs = (
        P(None, ("tx", "ty", "solver")),
        P(("tx", "ty", "solver")),
        P("tx", "ty", "solver", None, None, None),
        P("tx", "ty", "solver", None, None),
        P("tx", "ty", "solver", None),
        P("tx", "ty", "solver", None),
        P("tx", "ty", "solver"),
        P(None, "solver", "tx", "ty"),
        P(None, "solver", "tx", "ty"),
    )
    out_specs = (P(None, ("tx", "ty", "solver")), P(None, "solver", "tx", "ty"))
    return jax.shard_map(
        functools.partial(on_device, sizes), mesh=mesh, in_specs=in_specs, out_specs=out_specs, check_vma=False
    )
```
